32 devices in a mesh: dp: 4 (over z), space: 2 (over core), mp: 4 (over y, x).
Axes of the slice: x: 2, y: 2, z: 4, core: 2. Of those that a mesh axis runs over, the one named last changes fastest.
Arguments:
- features: bfloat16 [64, 64, 1024], P(('dp', 'space'), None, 'mp'), parts along dimension 0, may hold values from -6 to 6
- deconv_weight: bfloat16 [4, 512, 1024], P(None, 'mp'), may hold values from -0.1875 to 0.1875
- deconv_bias: float32 [512], P('mp'), may hold values from -3 to 3
- lateral_eight: bfloat16 [256, 512], P('mp'), may hold values from -0.25 to 0.25
- lateral_coarse: bfloat16 [2, 256, 1024], P(None, 'mp'), may hold values from -0.1875 to 0.1875
- output_conv: bfloat16 [3, 256, 9, 256], P(None, 'mp'), may hold values from -0.125 to 0.125
- norm_gain: float32 [6, 256], replicated, may hold values from 0.1 to 1.9
- norm_shift: float32 [6, 256], replicated, may hold values from -3 to 3
Outputs:
- level_eight: bfloat16 [256, 16384], P('mp', ('dp', 'space')), parts along dimension 1
- level_sixteen: bfloat16 [256, 4096], P('mp', ('dp', 'space')), parts along dimension 1
- level_thirty: bfloat16 [256, 1024], P('mp', ('dp', 'space')), parts along dimension 1
- level_sixty: bfloat16 [256, 256], P('mp', ('dp', 'space')), parts along dimension 1
The draws below stay inside these ranges and needn't reach their ends.
There are 4 independent parts, one for each index of `dp`. The reference program is written for one: setup_inputs(seed, part) draws one part's arguments, and reference() takes and returns one part's arrays. A program takes and returns all parts, laid end to end along the dimension named above; an argument that names none is the same for every part. Nothing has to cross between parts.
All inputs are finite; a program needn't handle non-finite values.
Results may differ from the reference program's by a relative error of at most 0.015.
Values may be sent and summed in bfloat16 or wider, within the bound.
A program may use at most 64 MiB of HBM per device.

```python
import jax
import jax.numpy as jnp
from jax import lax

D = 1024
NECK = 256
HALF = 512
COLS = 64
GRID = 16


def block_levels(stream_key, extent, split, least, high):
    gain = 1.0
    for axis_at, blocks in split:
        steps = jax.random.uniform(jax.random.fold_in(jax.random.fold_in(stream_key, 6), axis_at), (blocks,), jnp.float32, least / len(split), high / len(split))
        gain = gain * jnp.repeat(jnp.exp(steps), extent[axis_at] // blocks).reshape((-1,) + (1,) * (len(extent) - 1 - axis_at))
    return gain


def gaussian(key, extent, deviation, most, shards=(), held_as=jnp.bfloat16):
    loudness = block_levels(key, extent, shards, -0.22, 0.18) if shards else 1.0
    result = jax.random.normal(key, extent, jnp.float32) * deviation * loudness
    return jnp.minimum(jnp.maximum(result, -most), most).astype(held_as)


def setup_inputs(seed: int = 0, part: int = 0) -> dict:
    splits = jax.random.split(jax.random.key(seed), 9)
    own_keys = jax.random.split(jax.random.fold_in(splits[8], part), 9)
    return {
        "features": gaussian(own_keys[0], (GRID, COLS, D), 1.0, 6.0, ((0, 2), (2, 4))),
        "deconv_weight": gaussian(splits[1], (4, HALF, D), D ** -0.5, 0.1875, ((1, 4),)),
        "deconv_bias": gaussian(splits[2], (HALF,), 0.5, 3.0, ((0, 4),), jnp.float32),
        "lateral_eight": gaussian(splits[3], (NECK, HALF), HALF ** -0.5, 0.25, ((0, 4),)),
        "lateral_coarse": gaussian(splits[4], (2, NECK, D), D ** -0.5, 0.1875, ((1, 4),)),
        "output_conv": gaussian(splits[5], (3, NECK, 9, NECK), (9 * NECK) ** -0.5, 0.125, ((1, 4),)),
        "norm_gain": jnp.clip(1.0 + 0.18 * jax.random.normal(splits[6], (6, NECK), jnp.float32), 0.1, 1.9),
        "norm_shift": gaussian(splits[7], (6, NECK), 0.5, 3.0, (), jnp.float32),
    }


EPSILON = 1e-06

def channel_norm(values, gain_row, shift_row):
    floats = values.astype(jnp.float32)
    center = lax.optimization_barrier(jnp.mean(floats, axis=-1, keepdims=True))
    spread = lax.optimization_barrier(jnp.mean(floats * floats, axis=-1, keepdims=True)) - center * center
    scaled = (floats - center) * lax.rsqrt(spread + EPSILON)
    return (scaled * gain_row + shift_row).astype(jnp.bfloat16)

def conv_three(normed, weight):
    height, width, _ = normed.shape
    padded = jnp.pad(normed, ((1, 1), (1, 1), (0, 0)))
    totals = jnp.zeros((height * width, weight.shape[0]), jnp.float32)
    for tap_index in range(9):
        row_off = tap_index // 3
        col_off = tap_index % 3
        window = padded[row_off:row_off + height, col_off:col_off + width].reshape(height * width, -1)
        totals = totals + jnp.dot(window, weight[:, tap_index, :].T, preferred_element_type=jnp.float32)
    return totals.reshape(height, width, -1).astype(jnp.bfloat16)

def pool_pairs(values):
    height, width, depth = values.shape
    return lax.optimization_barrier(jnp.max(values.reshape(height // 2, 2, width // 2, 2, depth), axis=(1, 3)))

def channel_major(values):
    return values.transpose(2, 0, 1).reshape(values.shape[2], -1)

def reference(features, deconv_weight, deconv_bias, lateral_eight, lateral_coarse, output_conv, norm_gain, norm_shift):
    height, width, depth = features.shape
    half_width = deconv_weight.shape[1]
    flattened = features.reshape(height * width, depth)
    raised = jnp.dot(flattened, deconv_weight.reshape(4 * half_width, depth).T, preferred_element_type=jnp.float32)
    raised = raised.reshape(height, width, 2, 2, half_width) + deconv_bias
    upsampled = raised.transpose(0, 2, 1, 3, 4).reshape(2 * height, 2 * width, half_width).astype(jnp.bfloat16)
    pooled = pool_pairs(features)
    lat_a = jnp.dot(upsampled.reshape(-1, half_width), lateral_eight.T, preferred_element_type=jnp.float32)
    lat_a = lat_a.reshape(2 * height, 2 * width, -1).astype(jnp.bfloat16)
    lat_b = jnp.dot(flattened, lateral_coarse[0].T, preferred_element_type=jnp.float32)
    lat_b = lat_b.reshape(height, width, -1).astype(jnp.bfloat16)
    lat_c = jnp.dot(pooled.reshape(-1, depth), lateral_coarse[1].T, preferred_element_type=jnp.float32)
    lat_c = lat_c.reshape(height // 2, width // 2, -1).astype(jnp.bfloat16)
    results = []
    for level_index, lateral in enumerate((lat_a, lat_b, lat_c)):
        normed = channel_norm(lateral, norm_gain[2 * level_index], norm_shift[2 * level_index])
        convolved = conv_three(normed, output_conv[level_index])
        results.append(channel_norm(convolved, norm_gain[2 * level_index + 1], norm_shift[2 * level_index + 1]))
    level_sixty = results[2][::2, ::2]
    return (channel_major(results[0]), channel_major(results[1]), channel_major(results[2]), channel_major(level_sixty))
```

```python
import functools

import jax
import jax.numpy as jnp
from jax import lax
from jax.experimental import pallas as pl
from jax.experimental.pallas import tpu as pltpu
from jax.sharding import PartitionSpec as P

EPSILON = 1e-06
MESH = pl.DeviceIdType.MESH


def extended(block, sides, width):
    for axis, dim in sides:
        count = lax.axis_size(axis)
        forward = [(i, i + 1) for i in range(count - 1)]
        backward = [(target, source) for source, target in forward]
        low = lax.ppermute(
            lax.slice_in_dim(block, block.shape[dim] - width, None, axis=dim), axis, forward
        )
        high = lax.ppermute(lax.slice_in_dim(block, 0, width, axis=dim), axis, backward)
        block = jnp.concatenate([low, block, high], axis=dim)
    return block


def pool_pairs(values):
    height, width, depth = values.shape
    return jnp.max(values.reshape(height // 2, 2, width // 2, 2, depth), axis=(1, 3))


def contract_last(weight_rows, data):
    return lax.dot_general(
        weight_rows, data, (((1,), (1,)), ((), ())), preferred_element_type=jnp.float32
    )


def apply_norm(values, sums, squares, neck_width, gain_row, shift_row):
    floats = values.astype(jnp.float32)
    center = (sums / neck_width)[None, :]
    spread = (squares / neck_width)[None, :] - center * center
    scaled = (floats - center) * lax.rsqrt(spread + EPSILON)
    return (scaled * gain_row[:, None] + shift_row[:, None]).astype(jnp.bfloat16)


def cell_moments(values):
    floats = values.astype(jnp.float32)
    return (jnp.sum(floats, axis=0), jnp.sum(floats * floats, axis=0))


def conv_taps(totals, padded, weight, height, width):
    depth = padded.shape[0]
    for tap_index in range(9):
        row_off = tap_index // 3
        col_off = tap_index % 3
        window = padded[:, row_off : row_off + height, col_off : col_off + width].reshape(
            depth, height * width
        )
        rows_used = weight[:, tap_index, :]
        totals = totals + jnp.dot(rows_used, window, preferred_element_type=jnp.float32)
    return totals


def pyramid_level(lateral, height, width, level_index, output_conv, norm_gain, norm_shift):
    local_ch = lateral.shape[0]
    neck_width = local_ch * lax.axis_size("mp")
    own_first = lax.axis_index("mp") * local_ch
    weight = output_conv[level_index]
    initial = jnp.zeros((local_ch, height * width), jnp.float32)
    gathered = lax.all_gather(lateral, "mp", axis=0, tiled=True)
    sums, squares = cell_moments(gathered)
    normed = apply_norm(
        gathered, sums, squares, neck_width, norm_gain[2 * level_index], norm_shift[2 * level_index]
    )
    rimmed = extended(normed.reshape(neck_width, height, width), (("space", 1),), 1)
    padded = jnp.pad(rimmed, ((0, 0), (0, 0), (1, 1)))
    conv_out = conv_taps(initial, padded, weight, height, width)
    convolved = conv_out.astype(jnp.bfloat16)
    sums, squares = lax.psum(cell_moments(convolved), "mp")
    gain_row = lax.dynamic_slice_in_dim(norm_gain[2 * level_index + 1], own_first, local_ch, 0)
    shift_row = lax.dynamic_slice_in_dim(norm_shift[2 * level_index + 1], own_first, local_ch, 0)
    return apply_norm(convolved, sums, squares, neck_width, gain_row, shift_row)


def channel_pyramid(
    features,
    deconv_weight,
    deconv_bias,
    lateral_eight,
    lateral_coarse,
    output_conv,
    norm_gain,
    norm_shift,
):
    row_count, col_count, _ = features.shape
    half_local = deconv_weight.shape[1]
    neck_local = lateral_coarse.shape[1]
    pixels = row_count * col_count
    coarse_pixels = row_count // 2 * (col_count // 2)
    deconv_flat = deconv_weight.reshape(4 * half_local, deconv_weight.shape[2])
    piece = lax.all_gather(features, "mp", axis=2, tiled=True)
    depth = piece.shape[2]
    flattened = piece.reshape(pixels, depth)
    raised = contract_last(deconv_flat, flattened)
    middle = contract_last(lateral_coarse[0], flattened)
    pooled_flat = pool_pairs(piece).reshape(coarse_pixels, depth)
    coarse = contract_last(lateral_coarse[1], pooled_flat)
    raised, middle, coarse = (raised, middle, coarse)
    raised = (
        raised.reshape(2, 2, half_local, row_count, col_count)
        + deconv_bias[None, None, :, None, None]
    )
    upsampled = raised.transpose(2, 3, 0, 4, 1).reshape(half_local, 4 * pixels).astype(jnp.bfloat16)
    piece = lax.all_gather(upsampled, "mp", axis=0, tiled=True)
    lateral_sum = jnp.dot(lateral_eight, piece, preferred_element_type=jnp.float32)
    lat_eight = lateral_sum.astype(jnp.bfloat16)
    lat_sixteen = middle.astype(jnp.bfloat16)
    lat_thirty = coarse.astype(jnp.bfloat16)
    level_eight = pyramid_level(
        lat_eight, 2 * row_count, 2 * col_count, 0, output_conv, norm_gain, norm_shift
    )
    level_sixteen = pyramid_level(
        lat_sixteen, row_count, col_count, 1, output_conv, norm_gain, norm_shift
    )
    level_thirty = pyramid_level(
        lat_thirty, row_count // 2, col_count // 2, 2, output_conv, norm_gain, norm_shift
    )
    level_sixty = level_thirty.reshape(neck_local, row_count // 2, col_count // 2)[
        :, ::2, ::2
    ].reshape(neck_local, -1)
    return (level_eight, level_sixteen, level_thirty, level_sixty)


def nt(left, right):
    return lax.dot_general(
        left, right, (((1,), (1,)), ((), ())), preferred_element_type=jnp.float32
    )


def lane_norm(values, gain_row, shift_row):
    floats = values.astype(jnp.float32)
    center = jnp.mean(floats, axis=1, keepdims=True)
    spread = jnp.mean(floats * floats, axis=1, keepdims=True) - center * center
    scaled = (floats - center) * lax.rsqrt(spread + EPSILON)
    return scaled * gain_row + shift_row


def shifted(values, step, cols):
    count = values.shape[0]
    moved = pltpu.roll(values, step % count, 0)
    col = lax.rem(lax.broadcasted_iota(jnp.int32, values.shape, 0), cols)
    edge = 0 if step > 0 else cols - 1
    return jnp.where(col == edge, 0.0, moved)


FEAT, LATW, CONVW, RAISE, COARSE, MOMENT, FINAL = range(7)
KINDS = 7


def pyramid_kernel(
    n, bands, rows, cols, neck, half,
    feat, dw, bias, lat, lc, oc, gain, shift, gcol, scol,
    o8, o16, o32, o64,
    fbuf, dwv, lcv, latw, w0, w1, w2, acc, pool, ubuf, usend, cbuf, v8, x16, x32,
    halo8, halo16, halo32, send8, send16, send32, mbuf, inter, osend,
    ssem, rsem, lsem, hs, hr,
):
    me = lax.axis_index("mp")
    band = lax.axis_index("space")
    depth = feat.shape[1]
    own = neck // n
    hown = half // n
    px = rows * cols
    prows = rows // n
    part = prows * cols
    nine = 9 * neck
    r2, c2 = rows // 2, cols // 2
    px2 = r2 * c2

    def at_mp(k):
        return lax.rem(me + k, n)

    locals_ = [
        pltpu.make_async_copy(feat, fbuf.at[0], lsem.at[0]),
        pltpu.make_async_copy(dw, dwv, lsem.at[1]),
        pltpu.make_async_copy(lc, lcv, lsem.at[2]),
        pltpu.make_async_copy(lat, latw.at[pl.ds(pl.multiple_of(me * own, own), own)], lsem.at[3]),
        pltpu.make_async_copy(oc.at[0], w0.at[pl.ds(pl.multiple_of(me * own, own), own)], lsem.at[4]),
        pltpu.make_async_copy(oc.at[1], w1, lsem.at[5]),
        pltpu.make_async_copy(oc.at[2], w2, lsem.at[6]),
    ]
    for copy in locals_:
        copy.start()

    barrier = pltpu.get_barrier_semaphore()
    for b in range(bands):
        for k in range(n):
            if b == 0 and k == 0:
                continue
            pl.semaphore_signal(
                barrier,
                inc=1,
                device_id={"space": lax.rem(band + b, bands), "mp": at_mp(k)},
                device_id_type=MESH,
            )
    pl.semaphore_wait(barrier, bands * n - 1)

    def remote(src, dst, kind, k):
        return pltpu.make_async_remote_copy(
            src_ref=src,
            dst_ref=dst,
            send_sem=ssem.at[kind, k],
            recv_sem=rsem.at[kind, k],
            device_id={"mp": at_mp(k)},
            device_id_type=MESH,
        )

    peers = list(range(1, n))
    mine = pl.ds(pl.multiple_of(me * own, own), own)
    sends = {}

    def launch(kind, make):
        for k in peers:
            copy = remote(*make(k), kind, k)
            copy.start()
            sends[kind, k] = copy

    launch(FEAT, lambda k: (feat, fbuf.at[k]))
    launch(LATW, lambda k: (lat, latw.at[mine]))

    lat16 = jnp.zeros((own, px), jnp.float32)
    lat32 = jnp.zeros((own, px2), jnp.float32)
    for k in range(n):
        if k == 0:
            for i in range(3):
                locals_[i].wait()
        else:
            sends[FEAT, k].wait_recv()
        src = lax.rem(me - k + n, n)
        span = pl.ds(pl.multiple_of(src * depth, depth), depth)
        block = fbuf[k]
        term = nt(block, dwv[:, span])
        if k == 0:
            acc[...] = term
        else:
            acc[...] += term
        lat16 = lat16 + nt(lcv[0:own, span], block)
        floats = block.astype(jnp.float32).reshape(r2, 2 * cols, depth)
        tall = jnp.maximum(floats[:, :cols], floats[:, cols:]).reshape(r2 * cols, depth)
        halves = []
        for g in range(depth // 128):
            pool[...] = tall[:, g * 128 : (g + 1) * 128]
            halves.append(jnp.maximum(pool[pl.ds(0, px2, stride=2), :], pool[pl.ds(1, px2, stride=2), :]))
        pooled = jnp.concatenate(halves, axis=1).astype(jnp.bfloat16)
        lat32 = lat32 + nt(lcv[own:, span], pooled)

    for d in range(n):
        for il in range(prows):
            base = (d * prows + il) * cols
            for a in range(2):
                for b in range(2):
                    tap = 2 * a + b
                    value = acc[base : base + cols, tap * hown : (tap + 1) * hown] + bias[...]
                    at = (b * 2 * prows + 2 * il + a) * cols
                    usend[d, at : at + cols, :] = value.astype(jnp.bfloat16)
    launch(RAISE, lambda k: (usend.at[at_mp(k)], ubuf.at[k]))
    cbuf[mine, 0:px] = lat16.astype(jnp.bfloat16)
    cbuf[mine, px:] = lat32.astype(jnp.bfloat16)
    launch(COARSE, lambda k: (cbuf.at[mine], cbuf.at[mine]))
    locals_[4].wait()
    launch(CONVW, lambda k: (oc.at[0], w0.at[mine]))

    locals_[3].wait()
    for k in peers:
        sends[LATW, k].wait_recv()
    total = nt(usend[me], latw[:, pl.ds(pl.multiple_of(me * hown, hown), hown)])
    for k in peers:
        sends[RAISE, k].wait_recv()
        src = lax.rem(me - k + n, n)
        total = total + nt(ubuf[k], latw[:, pl.ds(pl.multiple_of(src * hown, hown), hown)])
    own_rows = 2 * prows
    wide = own_rows * cols
    normed = lane_norm(total.astype(jnp.bfloat16), gain[0:1, :], shift[0:1, :])
    rounded = normed.astype(jnp.bfloat16)
    for b in range(2):
        send8[0, b * cols : (b + 1) * cols, :] = rounded[b * wide : b * wide + cols]
        send8[1, b * cols : (b + 1) * cols, :] = rounded[(b + 1) * wide - cols : (b + 1) * wide]

    place = band * n + me
    last = bands * n - 1

    def halo(src_buf, dst_buf, level, low_if, low_dev, high_if, high_dev):
        low = pltpu.make_async_remote_copy(
            src_ref=src_buf.at[0], dst_ref=dst_buf.at[1], send_sem=hs.at[level, 0],
            recv_sem=hr.at[level, 1], device_id=low_dev, device_id_type=MESH)
        high = pltpu.make_async_remote_copy(
            src_ref=src_buf.at[1], dst_ref=dst_buf.at[0], send_sem=hs.at[level, 1],
            recv_sem=hr.at[level, 0], device_id=high_dev, device_id_type=MESH)

        @pl.when(low_if)
        def _():
            low.start()

        @pl.when(high_if)
        def _():
            high.start()

        def finish():
            @pl.when(low_if)
            def _():
                low.wait_send()
                high_like = pltpu.make_async_remote_copy(
                    src_ref=src_buf.at[1], dst_ref=dst_buf.at[0], send_sem=hs.at[level, 1],
                    recv_sem=hr.at[level, 0], device_id=low_dev, device_id_type=MESH)
                high_like.wait_recv()

            @pl.when(high_if)
            def _():
                high.wait_send()
                low_like = pltpu.make_async_remote_copy(
                    src_ref=src_buf.at[0], dst_ref=dst_buf.at[1], send_sem=hs.at[level, 0],
                    recv_sem=hr.at[level, 1], device_id=high_dev, device_id_type=MESH)
                low_like.wait_recv()

            @pl.when(jnp.logical_not(low_if))
            def _():
                dst_buf[0] = jnp.zeros(dst_buf.shape[1:], dst_buf.dtype)

            @pl.when(jnp.logical_not(high_if))
            def _():
                dst_buf[1] = jnp.zeros(dst_buf.shape[1:], dst_buf.dtype)

        return finish

    def device_of(index):
        return {"space": lax.div(index, n), "mp": lax.rem(index, n)}

    finish8 = halo(
        send8, halo8, 0,
        place > 0, device_of(jnp.maximum(place - 1, 0)),
        place < last, device_of(jnp.minimum(place + 1, last)),
    )
    zero = normed[0:wide]
    one = normed[wide:]

    def fill8(at, count, even, odd):
        v8[0, at : at + count, :] = shifted(odd, 1, cols).astype(jnp.bfloat16)
        v8[1, at : at + count, :] = even.astype(jnp.bfloat16)
        v8[2, at : at + count, :] = odd.astype(jnp.bfloat16)
        v8[3, at : at + count, :] = shifted(even, -1, cols).astype(jnp.bfloat16)

    fill8(cols, wide, zero, one)

    for k in peers:
        sends[COARSE, k].wait_recv()
    coarse = cbuf[...].astype(jnp.float32).T
    levels = (
        (1, rows, cols, x16, send16, halo16, w1, coarse[:px], 0),
        (2, r2, c2, x32, send32, halo32, w2, coarse[px:], px),
    )

    def fill(x, at, count, values, width):
        x[0, at : at + count, :] = shifted(values, 1, width).astype(jnp.bfloat16)
        x[1, at : at + count, :] = values.astype(jnp.bfloat16)
        x[2, at : at + count, :] = shifted(values, -1, width).astype(jnp.bfloat16)

    finishes = []
    for level, height, width, x, snd, hal, w, values, at in levels:
        out = lane_norm(values, gain[2 * level : 2 * level + 1, :], shift[2 * level : 2 * level + 1, :])
        fill(x, width, height * width, out, width)
        snd[0] = out[:width].astype(jnp.bfloat16)
        snd[1] = out[height * width - width :].astype(jnp.bfloat16)
        finishes.append(halo(
            snd, hal, level,
            band > 0, {"space": jnp.maximum(band - 1, 0)},
            band < bands - 1, {"space": jnp.minimum(band + 1, bands - 1)},
        ))
    maps = []
    locals_[5].wait()
    locals_[6].wait()
    for (level, height, width, x, snd, hal, w, values, at), done in zip(levels, finishes):
        done()
        fill(x, 0, width, hal[0].astype(jnp.float32), width)
        fill(x, (height + 1) * width, width, hal[1].astype(jnp.float32), width)
        result = jnp.zeros((own, height * width), jnp.float32)
        for tap in range(9):
            r, q = tap // 3, tap % 3
            result = result + nt(
                w[:, tap * neck : (tap + 1) * neck], x[q, r * width : (r + height) * width, :]
            )
        result = result.astype(jnp.bfloat16).astype(jnp.float32)
        span = slice(at, at + height * width)
        mbuf[0, 0:1, span] = jnp.sum(result, axis=0, keepdims=True)
        mbuf[0, 1:2, span] = jnp.sum(result * result, axis=0, keepdims=True)
        maps.append(result)
    launch(MOMENT, lambda k: (mbuf.at[0], mbuf.at[k]))

    finish8()
    fill8(0, cols, halo8[0, 0:cols].astype(jnp.float32), halo8[0, cols:].astype(jnp.float32))
    fill8(cols + wide, cols, halo8[1, 0:cols].astype(jnp.float32), halo8[1, cols:].astype(jnp.float32))
    for k in peers:
        sends[CONVW, k].wait_recv()
    for b in range(2):
        result = jnp.zeros((wide, neck), jnp.float32)
        for tap in range(9):
            r, q = tap // 3, tap % 3
            result = result + nt(
                v8[b + q, r * cols : r * cols + wide, :], w0[:, tap * neck : (tap + 1) * neck]
            )
        out = lane_norm(result.astype(jnp.bfloat16), gain[1:2, :], shift[1:2, :])
        for g in range(neck // 128):
            inter[g, pl.ds(b, wide, stride=2), :] = out[:, g * 128 : (g + 1) * 128]
    for g in range(neck // 128):
        osend[g * 128 : (g + 1) * 128, :] = inter[g].T.astype(jnp.bfloat16)
    cells = pl.ds(pl.multiple_of(me * 2 * wide, 2 * wide), 2 * wide)
    launch(FINAL, lambda k: (osend.at[pl.ds(pl.multiple_of(at_mp(k) * own, own), own)], o8.at[:, cells]))
    o8[:, cells] = osend[mine, :]

    for k in peers:
        sends[MOMENT, k].wait_recv()
    moments = mbuf[0]
    for k in peers:
        moments = moments + mbuf[k]
    moments = moments / neck
    for (level, height, width, x, snd, hal, w, values, at), result in zip(levels, maps):
        span = slice(at, at + height * width)
        center = moments[0:1, span]
        spread = moments[1:2, span] - center * center
        scaled = (result - center) * lax.rsqrt(spread + EPSILON)
        final = (scaled * gcol[:, level : level + 1] + scol[:, level : level + 1]).astype(jnp.bfloat16)
        if level == 1:
            o16[...] = final
        else:
            o32[...] = final
            count = o64.shape[1]
            wide2 = c2 // 2
            cell = lax.broadcasted_iota(jnp.int32, (px2, count), 0)
            target = lax.broadcasted_iota(jnp.int32, (px2, count), 1)
            wanted = lax.div(target, wide2) * (2 * c2) + 2 * lax.rem(target, wide2)
            pick = jnp.where(cell == wanted, 1.0, 0.0).astype(jnp.bfloat16)
            o64[...] = jnp.dot(final, pick, preferred_element_type=jnp.float32).astype(jnp.bfloat16)

    for kind in range(KINDS):
        for k in peers:
            sends[kind, k].wait_send()
    for k in peers:
        sends[FINAL, k].wait_recv()


def fused(features, deconv_weight, deconv_bias, lateral_eight, lateral_coarse, output_conv,
          norm_gain, norm_shift):
    n = lax.axis_size("mp")
    bands = lax.axis_size("space")
    rows, cols, depth = features.shape
    full = deconv_weight.shape[2]
    hown = deconv_weight.shape[1]
    own = lateral_eight.shape[0]
    neck, half = own * n, hown * n
    px, px2 = rows * cols, rows * cols // 4
    wide = 2 * (rows // n) * cols
    first = lax.axis_index("mp") * own
    gcol = lax.dynamic_slice_in_dim(norm_gain[1::2], first, own, 1).T
    scol = lax.dynamic_slice_in_dim(norm_shift[1::2], first, own, 1).T
    bf, f32 = jnp.bfloat16, jnp.float32
    vmem = pl.BlockSpec(memory_space=pltpu.VMEM)
    hbm = pl.BlockSpec(memory_space=pl.ANY)
    shapes = [
        ((n, px, depth), bf), ((4 * hown, full), bf), ((2 * own, full), bf),
        ((neck, half), bf), ((neck, 9 * neck), bf), ((own, 9 * neck), bf), ((own, 9 * neck), bf),
        ((px, 4 * hown), f32), ((px // 2, 128), f32), ((n, 2 * wide, hown), bf),
        ((n, 2 * wide, hown), bf), ((neck, px + px2), bf),
        ((4, wide + 2 * cols, neck), bf), ((3, px + 2 * cols, neck), bf),
        ((3, px2 + cols, neck), bf),
        ((2, 2 * cols, neck), bf), ((2, cols, neck), bf), ((2, cols // 2, neck), bf),
        ((2, 2 * cols, neck), bf), ((2, cols, neck), bf), ((2, cols // 2, neck), bf),
        ((n, 8, px + px2), f32), ((neck // 128, 2 * wide, 128), f32), ((neck, 2 * wide), bf),
    ]
    return pl.pallas_call(
        functools.partial(pyramid_kernel, n, bands, rows, cols, neck, half),
        out_shape=[
            jax.ShapeDtypeStruct((own, 4 * px), bf), jax.ShapeDtypeStruct((own, px), bf),
            jax.ShapeDtypeStruct((own, px2), bf), jax.ShapeDtypeStruct((own, px2 // 4), bf),
        ],
        in_specs=[hbm, hbm, vmem, hbm, hbm, hbm, vmem, vmem, vmem, vmem],
        out_specs=[vmem] * 4,
        scratch_shapes=[pltpu.VMEM(s, d) for s, d in shapes] + [
            pltpu.SemaphoreType.DMA((KINDS, n)), pltpu.SemaphoreType.DMA((KINDS, n)),
            pltpu.SemaphoreType.DMA((7,)), pltpu.SemaphoreType.DMA((3, 2)),
            pltpu.SemaphoreType.DMA((3, 2)),
        ],
        compiler_params=pltpu.CompilerParams(
            collective_id=0, has_side_effects=True, vmem_limit_bytes=56 << 20
        ),
    )(
        features.reshape(px, depth), deconv_weight.reshape(4 * hown, full),
        deconv_bias.reshape(1, hown), lateral_eight, lateral_coarse.reshape(2 * own, full),
        output_conv.reshape(3, own, 9 * neck), norm_gain, norm_shift, gcol, scol,
    )


def per_device(features, deconv_weight, *rest):
    n = lax.axis_size("mp")
    rows, cols, depth = features.shape
    aligned = depth % 128 == 0 and deconv_weight.shape[1] % 128 == 0
    if aligned and rows % n == 0 and rows % 4 == 0 and cols % 64 == 0:
        return tuple(fused(features, deconv_weight, *rest))
    return channel_pyramid(features, deconv_weight, *rest)


def solution(mesh):
    return jax.shard_map(
        per_device,
        mesh=mesh,
        in_specs=(
            P(("dp", "space"), None, "mp"),
            P(None, "mp", None),
            P("mp"),
            P("mp", None),
            P(None, "mp", None),
            P(None, "mp", None, None),
            P(),
            P(),
        ),
        out_specs=(
            P("mp", ("dp", "space")),
            P("mp", ("dp", "space")),
            P("mp", ("dp", "space")),
            P("mp", ("dp", "space")),
        ),
        check_vma=False,
    )
```

```python
import functools

import jax
import jax.numpy as jnp
from jax import lax
from jax.experimental import pallas as pl
from jax.experimental.pallas import tpu as pltpu
from jax.sharding import PartitionSpec as P

EPSILON = 1e-06
MESH = pl.DeviceIdType.MESH


def extended(block, sides, width):
    for axis, dim in sides:
        count = lax.axis_size(axis)
        forward = [(i, i + 1) for i in range(count - 1)]
        backward = [(target, source) for source, target in forward]
        low = lax.ppermute(
            lax.slice_in_dim(block, block.shape[dim] - width, None, axis=dim), axis, forward
        )
        high = lax.ppermute(lax.slice_in_dim(block, 0, width, axis=dim), axis, backward)
        block = jnp.concatenate([low, block, high], axis=dim)
    return block


def pool_pairs(values):
    height, width, depth = values.shape
    return jnp.max(values.reshape(height // 2, 2, width // 2, 2, depth), axis=(1, 3))


def contract_last(weight_rows, data):
    return lax.dot_general(
        weight_rows, data, (((1,), (1,)), ((), ())), preferred_element_type=jnp.float32
    )


def apply_norm(values, sums, squares, neck_width, gain_row, shift_row):
    floats = values.astype(jnp.float32)
    center = (sums / neck_width)[None, :]
    spread = (squares / neck_width)[None, :] - center * center
    scaled = (floats - center) * lax.rsqrt(spread + EPSILON)
    return (scaled * gain_row[:, None] + shift_row[:, None]).astype(jnp.bfloat16)


def cell_moments(values):
    floats = values.astype(jnp.float32)
    return (jnp.sum(floats, axis=0), jnp.sum(floats * floats, axis=0))


def conv_taps(totals, padded, weight, height, width):
    depth = padded.shape[0]
    for tap_index in range(9):
        row_off = tap_index // 3
        col_off = tap_index % 3
        window = padded[:, row_off : row_off + height, col_off : col_off + width].reshape(
            depth, height * width
        )
        rows_used = weight[:, tap_index, :]
        totals = totals + jnp.dot(rows_used, window, preferred_element_type=jnp.float32)
    return totals


def pyramid_level(lateral, height, width, level_index, output_conv, norm_gain, norm_shift):
    local_ch = lateral.shape[0]
    neck_width = local_ch * lax.axis_size("mp")
    own_first = lax.axis_index("mp") * local_ch
    weight = output_conv[level_index]
    initial = jnp.zeros((local_ch, height * width), jnp.float32)
    gathered = lax.all_gather(lateral, "mp", axis=0, tiled=True)
    sums, squares = cell_moments(gathered)
    normed = apply_norm(
        gathered, sums, squares, neck_width, norm_gain[2 * level_index], norm_shift[2 * level_index]
    )
    rimmed = extended(normed.reshape(neck_width, height, width), (("space", 1),), 1)
    padded = jnp.pad(rimmed, ((0, 0), (0, 0), (1, 1)))
    conv_out = conv_taps(initial, padded, weight, height, width)
    convolved = conv_out.astype(jnp.bfloat16)
    sums, squares = lax.psum(cell_moments(convolved), "mp")
    gain_row = lax.dynamic_slice_in_dim(norm_gain[2 * level_index + 1], own_first, local_ch, 0)
    shift_row = lax.dynamic_slice_in_dim(norm_shift[2 * level_index + 1], own_first, local_ch, 0)
    return apply_norm(convolved, sums, squares, neck_width, gain_row, shift_row)


def channel_pyramid(
    features,
    deconv_weight,
    deconv_bias,
    lateral_eight,
    lateral_coarse,
    output_conv,
    norm_gain,
    norm_shift,
):
    row_count, col_count, _ = features.shape
    half_local = deconv_weight.shape[1]
    neck_local = lateral_coarse.shape[1]
    pixels = row_count * col_count
    coarse_pixels = row_count // 2 * (col_count // 2)
    deconv_flat = deconv_weight.reshape(4 * half_local, deconv_weight.shape[2])
    piece = lax.all_gather(features, "mp", axis=2, tiled=True)
    depth = piece.shape[2]
    flattened = piece.reshape(pixels, depth)
    raised = contract_last(deconv_flat, flattened)
    middle = contract_last(lateral_coarse[0], flattened)
    pooled_flat = pool_pairs(piece).reshape(coarse_pixels, depth)
    coarse = contract_last(lateral_coarse[1], pooled_flat)
    raised, middle, coarse = (raised, middle, coarse)
    raised = (
        raised.reshape(2, 2, half_local, row_count, col_count)
        + deconv_bias[None, None, :, None, None]
    )
    upsampled = raised.transpose(2, 3, 0, 4, 1).reshape(half_local, 4 * pixels).astype(jnp.bfloat16)
    piece = lax.all_gather(upsampled, "mp", axis=0, tiled=True)
    lateral_sum = jnp.dot(lateral_eight, piece, preferred_element_type=jnp.float32)
    lat_eight = lateral_sum.astype(jnp.bfloat16)
    lat_sixteen = middle.astype(jnp.bfloat16)
    lat_thirty = coarse.astype(jnp.bfloat16)
    level_eight = pyramid_level(
        lat_eight, 2 * row_count, 2 * col_count, 0, output_conv, norm_gain, norm_shift
    )
    level_sixteen = pyramid_level(
        lat_sixteen, row_count, col_count, 1, output_conv, norm_gain, norm_shift
    )
    level_thirty = pyramid_level(
        lat_thirty, row_count // 2, col_count // 2, 2, output_conv, norm_gain, norm_shift
    )
    level_sixty = level_thirty.reshape(neck_local, row_count // 2, col_count // 2)[
        :, ::2, ::2
    ].reshape(neck_local, -1)
    return (level_eight, level_sixteen, level_thirty, level_sixty)


def nt(left, right):
    return lax.dot_general(
        left, right, (((1,), (1,)), ((), ())), preferred_element_type=jnp.float32
    )


def lane_norm(values, gain_row, shift_row):
    floats = values.astype(jnp.float32)
    center = jnp.mean(floats, axis=1, keepdims=True)
    spread = jnp.mean(floats * floats, axis=1, keepdims=True) - center * center
    scaled = (floats - center) * lax.rsqrt(spread + EPSILON)
    return scaled * gain_row + shift_row


def shifted(values, step, cols):
    count = values.shape[0]
    moved = pltpu.roll(values, step % count, 0)
    col = lax.rem(lax.broadcasted_iota(jnp.int32, values.shape, 0), cols)
    edge = 0 if step > 0 else cols - 1
    return jnp.where(col == edge, 0.0, moved)


FEAT, RAISE, COARSE, MOMENT, FINAL = range(5)
KINDS = 5


def pyramid_kernel(
    n, bands, rows, cols, neck, half,
    feat, dw, bias, lat, lc, oc, gain, shift,
    o8, o16, o32, o64,
    fbuf, dwv, lcv, latw, w0, w1, w2, acc, pool, ubuf, usend, cbuf, v8, x16, x32,
    halo8, halo16, halo32, send8, send16, send32, mbuf, inter, osend,
    ssem, rsem, lsem, hs, hr, fs, fr, ws, wr,
):
    me = lax.axis_index("mp")
    band = lax.axis_index("space")
    layer = lax.axis_index("dp")
    layers = lax.axis_size("dp")
    depth = feat.shape[1]
    own = neck // n
    hown = half // n
    px = rows * cols
    prows = rows // n
    part = prows * cols
    r2, c2 = rows // 2, cols // 2
    px2 = r2 * c2

    def at_mp(k):
        fast = lax.rem(lax.rem(me, 2) + k % 2, 2)
        slow = lax.rem(lax.div(me, 2) + k // 2, 2)
        return 2 * slow + fast

    locals_ = [
        pltpu.make_async_copy(feat, fbuf.at[0], lsem.at[0]),
        pltpu.make_async_copy(dw, dwv, lsem.at[1]),
        pltpu.make_async_copy(lc, lcv, lsem.at[2]),
        pltpu.make_async_copy(lat, latw.at[pl.ds(pl.multiple_of(me * own, own), own)], lsem.at[3]),
        pltpu.make_async_copy(oc.at[0], w0.at[:, pl.ds(pl.multiple_of(me * own, own), own)], lsem.at[4]),
        pltpu.make_async_copy(oc.at[1], w1, lsem.at[5]),
        pltpu.make_async_copy(oc.at[2], w2, lsem.at[6]),
    ]
    for copy in locals_:
        copy.start()

    barrier = pltpu.get_barrier_semaphore()
    for b in range(bands):
        for k in range(n):
            if b == 0 and k == 0:
                continue
            pl.semaphore_signal(
                barrier,
                inc=1,
                device_id={"space": lax.rem(band + b, bands), "mp": at_mp(k)},
                device_id_type=MESH,
            )
    for b in range(1, layers):
        pl.semaphore_signal(
            barrier, inc=1, device_id={"dp": lax.rem(layer + b, layers)}, device_id_type=MESH
        )
    pl.semaphore_wait(barrier, bands * n - 1 + layers - 1)

    def remote(src, dst, kind, k):
        return pltpu.make_async_remote_copy(
            src_ref=src,
            dst_ref=dst,
            send_sem=ssem.at[kind, k],
            recv_sem=rsem.at[kind, k],
            device_id={"mp": at_mp(k)},
            device_id_type=MESH,
        )

    peers = list(range(1, n))
    mine = pl.ds(pl.multiple_of(me * own, own), own)
    sends = {}

    def launch(kind, make):
        for k in peers:
            copy = remote(*make(k), kind, k)
            copy.start()
            sends[kind, k] = copy

    top = pl.ds(0, px // 2)
    low = pl.ds(px // 2, px // 2)

    def feature_copy(src, dst, slot, half_at, k):
        return pltpu.make_async_remote_copy(
            src_ref=src, dst_ref=dst, send_sem=fs.at[slot, half_at],
            recv_sem=fr.at[slot, half_at], device_id={"mp": at_mp(k)}, device_id_type=MESH)

    first = {}
    for k, half_at in ((1, 0), (2, 1), (1, 1), (2, 0)):
        span = (top, low)[half_at]
        first[k, half_at] = feature_copy(feat.at[span], fbuf.at[k, span], k, half_at, k)
    first[1, 0].start()
    first[2, 1].start()

    piece = own // layers
    taps = oc.shape[1]
    widths = (neck // bands, half // bands)

    def block(which, src, rows_at, count, ref, own_ref):
        lanes = pl.ds(pl.multiple_of(band * widths[which], widths[which]), widths[which])
        base = rows_at if own_ref else src * own + rows_at
        span = pl.ds(pl.multiple_of(base, count), count)
        if which == 0:
            return ref.at[0, :, span, lanes] if own_ref else ref.at[:, span, lanes]
        return ref.at[span, lanes]

    sources = (oc, lat)
    targets = (w0, latw)
    weight_sends = []
    stage_one, stage_two, stage_three = {}, {}, {}
    start_rows = layer * piece
    for which in (1, 0):
        for k in range(1, n):
            copy = pltpu.make_async_remote_copy(
                src_ref=block(which, me, start_rows, piece, sources[which], True),
                dst_ref=block(which, me, start_rows, piece, targets[which], False),
                send_sem=ws.at[which, 0, k], recv_sem=wr.at[which, 0, k],
                device_id={"mp": at_mp(k)}, device_id_type=MESH)
            copy.start()
            stage_one[which, k] = copy
    first[1, 1].start()
    first[2, 0].start()

    def share_along_dp():
        for which in (1, 0):
            for k in range(1, n):
                stage_one[which, k].wait_recv()
                for step in range(1, layers):
                    here = block(which, at_mp(k), start_rows, piece, targets[which], False)
                    copy = pltpu.make_async_remote_copy(
                        src_ref=here, dst_ref=here,
                        send_sem=ws.at[which, step, k], recv_sem=wr.at[which, step, k],
                        device_id={"dp": lax.rem(layer + step, layers)}, device_id_type=MESH)
                    copy.start()
                    stage_two[which, k, step] = copy

    def share_with_core(which):
        for k in range(1, n):
            for step in range(1, layers):
                stage_two[which, k, step].wait_recv()
            here = block(which, at_mp(k), 0, own, targets[which], False)
            copy = pltpu.make_async_remote_copy(
                src_ref=here, dst_ref=here,
                send_sem=ws.at[which, layers, k], recv_sem=wr.at[which, layers, k],
                device_id={"space": lax.rem(band + 1, bands)}, device_id_type=MESH)
            copy.start()
            stage_three[which, k] = copy

    lat16 = jnp.zeros((own, px), jnp.float32)
    lat32 = jnp.zeros((own, px2), jnp.float32)
    for k in range(n):
        if k == 0:
            for i in range(3):
                locals_[i].wait()
        elif k == 1:
            first[1, 0].wait_recv()
            relay = [feature_copy(fbuf.at[1, top], fbuf.at[3, top], 3, 0, 2)]
            relay[0].start()
            first[2, 1].wait_recv()
            relay.append(feature_copy(fbuf.at[2, low], fbuf.at[3, low], 3, 1, 1))
            relay[1].start()
            first[1, 1].wait_recv()
        elif k == 2:
            first[2, 0].wait_recv()
        else:
            share_along_dp()
            relay[0].wait_recv()
            relay[1].wait_recv()
        src = at_mp(k)
        span = pl.ds(pl.multiple_of(src * depth, depth), depth)
        values = fbuf[k]
        term = nt(values, dwv[:, span])
        if k == 0:
            acc[...] = term
        else:
            acc[...] += term
        lat16 = lat16 + nt(lcv[0:own, span], values)
        floats = values.astype(jnp.float32).reshape(r2, 2 * cols, depth)
        tall = jnp.maximum(floats[:, :cols], floats[:, cols:]).reshape(r2 * cols, depth)
        halves = []
        for g in range(depth // 128):
            pool[...] = tall[:, g * 128 : (g + 1) * 128]
            halves.append(jnp.maximum(pool[pl.ds(0, px2, stride=2), :], pool[pl.ds(1, px2, stride=2), :]))
        pooled = jnp.concatenate(halves, axis=1).astype(jnp.bfloat16)
        lat32 = lat32 + nt(lcv[own:, span], pooled)

    for d in range(n):
        for il in range(prows):
            base = (d * prows + il) * cols
            for a in range(2):
                for b in range(2):
                    tap = 2 * a + b
                    value = acc[base : base + cols, tap * hown : (tap + 1) * hown] + bias[...]
                    at = (b * 2 * prows + 2 * il + a) * cols
                    usend[d, at : at + cols, :] = value.astype(jnp.bfloat16)
    launch(RAISE, lambda k: (usend.at[at_mp(k)], ubuf.at[k]))
    cbuf[mine, 0:px] = lat16.astype(jnp.bfloat16)
    cbuf[mine, px:] = lat32.astype(jnp.bfloat16)
    launch(COARSE, lambda k: (cbuf.at[mine], cbuf.at[mine]))
    share_with_core(1)

    locals_[3].wait()
    for k in peers:
        stage_three[1, k].wait_recv()
    total = nt(usend[me], latw[:, pl.ds(pl.multiple_of(me * hown, hown), hown)])
    for k in peers:
        sends[RAISE, k].wait_recv()
        src = at_mp(k)
        total = total + nt(ubuf[k], latw[:, pl.ds(pl.multiple_of(src * hown, hown), hown)])
    own_rows = 2 * prows
    wide = own_rows * cols
    normed = lane_norm(total.astype(jnp.bfloat16), gain[0:1, :], shift[0:1, :])
    rounded = normed.astype(jnp.bfloat16)
    for b in range(2):
        send8[0, b * cols : (b + 1) * cols, :] = rounded[b * wide : b * wide + cols]
        send8[1, b * cols : (b + 1) * cols, :] = rounded[(b + 1) * wide - cols : (b + 1) * wide]

    place = band * n + me
    last = bands * n - 1

    def halo(src_buf, dst_buf, level, low_if, low_dev, high_if, high_dev):
        low = pltpu.make_async_remote_copy(
            src_ref=src_buf.at[0], dst_ref=dst_buf.at[1], send_sem=hs.at[level, 0],
            recv_sem=hr.at[level, 1], device_id=low_dev, device_id_type=MESH)
        high = pltpu.make_async_remote_copy(
            src_ref=src_buf.at[1], dst_ref=dst_buf.at[0], send_sem=hs.at[level, 1],
            recv_sem=hr.at[level, 0], device_id=high_dev, device_id_type=MESH)

        @pl.when(low_if)
        def _():
            low.start()

        @pl.when(high_if)
        def _():
            high.start()

        def finish():
            @pl.when(low_if)
            def _():
                low.wait_send()
                high_like = pltpu.make_async_remote_copy(
                    src_ref=src_buf.at[1], dst_ref=dst_buf.at[0], send_sem=hs.at[level, 1],
                    recv_sem=hr.at[level, 0], device_id=low_dev, device_id_type=MESH)
                high_like.wait_recv()

            @pl.when(high_if)
            def _():
                high.wait_send()
                low_like = pltpu.make_async_remote_copy(
                    src_ref=src_buf.at[0], dst_ref=dst_buf.at[1], send_sem=hs.at[level, 0],
                    recv_sem=hr.at[level, 1], device_id=high_dev, device_id_type=MESH)
                low_like.wait_recv()

            @pl.when(jnp.logical_not(low_if))
            def _():
                dst_buf[0] = jnp.zeros(dst_buf.shape[1:], dst_buf.dtype)

            @pl.when(jnp.logical_not(high_if))
            def _():
                dst_buf[1] = jnp.zeros(dst_buf.shape[1:], dst_buf.dtype)

        return finish

    def device_of(index):
        return {"space": lax.div(index, n), "mp": lax.rem(index, n)}

    finish8 = halo(
        send8, halo8, 0,
        place > 0, device_of(jnp.maximum(place - 1, 0)),
        place < last, device_of(jnp.minimum(place + 1, last)),
    )
    zero = normed[0:wide]
    one = normed[wide:]

    def fill8(at, count, even, odd):
        v8[0, at : at + count, :] = shifted(odd, 1, cols).astype(jnp.bfloat16)
        v8[1, at : at + count, :] = even.astype(jnp.bfloat16)
        v8[2, at : at + count, :] = odd.astype(jnp.bfloat16)
        v8[3, at : at + count, :] = shifted(even, -1, cols).astype(jnp.bfloat16)

    fill8(cols, wide, zero, one)

    share_with_core(0)
    for k in peers:
        sends[COARSE, k].wait_recv()
    coarse = cbuf[...].astype(jnp.float32).T
    levels = (
        (1, rows, cols, x16, send16, halo16, w1, coarse[:px], 0),
        (2, r2, c2, x32, send32, halo32, w2, coarse[px:], px),
    )

    def fill(x, at, count, values, width):
        x[0, at : at + count, :] = shifted(values, 1, width).astype(jnp.bfloat16)
        x[1, at : at + count, :] = values.astype(jnp.bfloat16)
        x[2, at : at + count, :] = shifted(values, -1, width).astype(jnp.bfloat16)

    finishes = []
    for level, height, width, x, snd, hal, w, values, at in levels:
        out = lane_norm(values, gain[2 * level : 2 * level + 1, :], shift[2 * level : 2 * level + 1, :])
        fill(x, width, height * width, out, width)
        snd[0] = out[:width].astype(jnp.bfloat16)
        snd[1] = out[height * width - width :].astype(jnp.bfloat16)
        finishes.append(halo(
            snd, hal, level,
            band > 0, {"space": jnp.maximum(band - 1, 0)},
            band < bands - 1, {"space": jnp.minimum(band + 1, bands - 1)},
        ))
    maps = []
    locals_[5].wait()
    locals_[6].wait()
    for (level, height, width, x, snd, hal, w, values, at), done in zip(levels, finishes):
        done()
        fill(x, 0, width, hal[0].astype(jnp.float32), width)
        fill(x, (height + 1) * width, width, hal[1].astype(jnp.float32), width)
        result = jnp.zeros((own, height * width), jnp.float32)
        for tap in range(9):
            r, q = tap // 3, tap % 3
            result = result + nt(
                w[tap], x[q, r * width : (r + height) * width, :]
            )
        result = result.astype(jnp.bfloat16).astype(jnp.float32)
        span = slice(at, at + height * width)
        mbuf[0, 0:1, span] = jnp.sum(result, axis=0, keepdims=True)
        mbuf[0, 1:2, span] = jnp.sum(result * result, axis=0, keepdims=True)
        maps.append(result)
    launch(MOMENT, lambda k: (mbuf.at[0], mbuf.at[k]))

    finish8()
    fill8(0, cols, halo8[0, 0:cols].astype(jnp.float32), halo8[0, cols:].astype(jnp.float32))
    fill8(cols + wide, cols, halo8[1, 0:cols].astype(jnp.float32), halo8[1, cols:].astype(jnp.float32))
    locals_[4].wait()
    for k in peers:
        stage_three[0, k].wait_recv()
    for b in range(2):
        result = jnp.zeros((wide, neck), jnp.float32)
        for tap in range(9):
            r, q = tap // 3, tap % 3
            result = result + nt(
                v8[b + q, r * cols : r * cols + wide, :], w0[tap]
            )
        out = lane_norm(result.astype(jnp.bfloat16), gain[1:2, :], shift[1:2, :])
        for g in range(neck // 128):
            inter[g, pl.ds(b, wide, stride=2), :] = out[:, g * 128 : (g + 1) * 128]
    for g in range(neck // 128):
        osend[g * 128 : (g + 1) * 128, :] = inter[g].T.astype(jnp.bfloat16)
    cells = pl.ds(pl.multiple_of(me * 2 * wide, 2 * wide), 2 * wide)
    launch(FINAL, lambda k: (osend.at[pl.ds(pl.multiple_of(at_mp(k) * own, own), own)], o8.at[:, cells]))
    o8[:, cells] = osend[mine, :]

    lane = lax.broadcasted_iota(jnp.int32, (own, neck), 1)
    row = lax.broadcasted_iota(jnp.int32, (own, neck), 0)
    chosen = lane == row + me * own

    def own_column(table, index):
        return jnp.sum(
            jnp.where(chosen, table[index : index + 1, :], 0.0), axis=1, keepdims=True
        )

    for k in peers:
        sends[MOMENT, k].wait_recv()
    moments = mbuf[0]
    for k in peers:
        moments = moments + mbuf[k]
    moments = moments / neck
    for (level, height, width, x, snd, hal, w, values, at), result in zip(levels, maps):
        span = slice(at, at + height * width)
        center = moments[0:1, span]
        spread = moments[1:2, span] - center * center
        scaled = (result - center) * lax.rsqrt(spread + EPSILON)
        final = (
            scaled * own_column(gain, 2 * level + 1) + own_column(shift, 2 * level + 1)
        ).astype(jnp.bfloat16)
        if level == 1:
            o16[...] = final
        else:
            o32[...] = final
            count = o64.shape[0]
            wide2 = c2 // 2
            cell = lax.broadcasted_iota(jnp.int32, (count, px2), 1)
            target = lax.broadcasted_iota(jnp.int32, (count, px2), 0)
            wanted = lax.div(target, wide2) * (2 * c2) + 2 * lax.rem(target, wide2)
            pick = jnp.where(cell == wanted, 1.0, 0.0).astype(jnp.bfloat16)
            o64[...] = nt(pick, final).astype(jnp.bfloat16)

    for copy in (*first.values(), *relay, *stage_one.values(), *stage_two.values(), *stage_three.values()):
        copy.wait_send()
    for kind in (RAISE, COARSE, MOMENT, FINAL):
        for k in peers:
            sends[kind, k].wait_send()
    for k in peers:
        sends[FINAL, k].wait_recv()


def fused(features, deconv_weight, deconv_bias, lateral_eight, lateral_coarse, output_conv,
          norm_gain, norm_shift):
    n = lax.axis_size("mp")
    bands = lax.axis_size("space")
    rows, cols, depth = features.shape
    full = deconv_weight.shape[2]
    hown = deconv_weight.shape[1]
    own = lateral_eight.shape[0]
    neck, half = own * n, hown * n
    layers = lax.axis_size("dp")
    px, px2 = rows * cols, rows * cols // 4
    wide = 2 * (rows // n) * cols
    bf, f32 = jnp.bfloat16, jnp.float32
    vmem = pl.BlockSpec(memory_space=pltpu.VMEM)
    hbm = pl.BlockSpec(memory_space=pl.ANY)
    shapes = [
        ((n, px, depth), bf), ((4 * hown, full), bf), ((2 * own, full), bf),
        ((neck, half), bf), ((9, neck, neck), bf), ((9, own, neck), bf), ((9, own, neck), bf),
        ((px, 4 * hown), f32), ((px // 2, 128), f32), ((n, 2 * wide, hown), bf),
        ((n, 2 * wide, hown), bf), ((neck, px + px2), bf),
        ((4, wide + 2 * cols, neck), bf), ((3, px + 2 * cols, neck), bf),
        ((3, px2 + cols, neck), bf),
        ((2, 2 * cols, neck), bf), ((2, cols, neck), bf), ((2, cols // 2, neck), bf),
        ((2, 2 * cols, neck), bf), ((2, cols, neck), bf), ((2, cols // 2, neck), bf),
        ((n, 8, px + px2), f32), ((neck // 128, 2 * wide, 128), f32), ((neck, 2 * wide), bf),
    ]
    eight, sixteen, thirty, sixty = pl.pallas_call(
        functools.partial(pyramid_kernel, n, bands, rows, cols, neck, half),
        out_shape=[
            jax.ShapeDtypeStruct((own, 4 * px), bf), jax.ShapeDtypeStruct((own, px), bf),
            jax.ShapeDtypeStruct((own, px2), bf), jax.ShapeDtypeStruct((px2 // 4, own), bf),
        ],
        in_specs=[hbm, hbm, vmem, hbm, hbm, hbm, vmem, vmem],
        out_specs=[vmem] * 4,
        scratch_shapes=[pltpu.VMEM(s, d) for s, d in shapes] + [
            pltpu.SemaphoreType.DMA((KINDS, n)), pltpu.SemaphoreType.DMA((KINDS, n)),
            pltpu.SemaphoreType.DMA((7,)), pltpu.SemaphoreType.DMA((3, 2)),
            pltpu.SemaphoreType.DMA((3, 2)),
            pltpu.SemaphoreType.DMA((n, 2)), pltpu.SemaphoreType.DMA((n, 2)),
            pltpu.SemaphoreType.DMA((2, layers + 1, n)), pltpu.SemaphoreType.DMA((2, layers + 1, n)),
        ],
        compiler_params=pltpu.CompilerParams(
            collective_id=0, has_side_effects=True, vmem_limit_bytes=56 << 20
        ),
    )(
        features.reshape(px, depth), deconv_weight.reshape(4 * hown, full),
        deconv_bias.reshape(1, hown), lateral_eight, lateral_coarse.reshape(2 * own, full),
        output_conv.transpose(0, 2, 1, 3), norm_gain, norm_shift,
    )
    return eight, sixteen, thirty, sixty.T


def per_device(features, deconv_weight, *rest):
    n = lax.axis_size("mp")
    rows, cols, depth = features.shape
    aligned = depth % 128 == 0 and deconv_weight.shape[1] % 128 == 0
    bands, layers = lax.axis_size("space"), lax.axis_size("dp")
    own, neck = rest[1].shape[0], rest[3].shape[3]
    aligned = aligned and n == 4 and bands == 2 and own % (16 * layers) == 0 and neck % (128 * bands) == 0
    if aligned and rows % n == 0 and rows % 4 == 0 and cols % 64 == 0:
        return tuple(fused(features, deconv_weight, *rest))
    return channel_pyramid(features, deconv_weight, *rest)


def solution(mesh):
    return jax.shard_map(
        per_device,
        mesh=mesh,
        in_specs=(
            P(("dp", "space"), None, "mp"),
            P(None, "mp", None),
            P("mp"),
            P("mp", None),
            P(None, "mp", None),
            P(None, "mp", None, None),
            P(),
            P(),
        ),
        out_specs=(
            P("mp", ("dp", "space")),
            P("mp", ("dp", "space")),
            P("mp", ("dp", "space")),
            P("mp", ("dp", "space")),
        ),
        check_vma=False,
    )
```

```python
import functools

import jax
import jax.numpy as jnp
from jax import lax
from jax.experimental import pallas as pl
from jax.experimental.pallas import tpu as pltpu
from jax.sharding import PartitionSpec as P

EPSILON = 1e-06
MESH = pl.DeviceIdType.MESH


def extended(block, sides, width):
    for axis, dim in sides:
        count = lax.axis_size(axis)
        forward = [(i, i + 1) for i in range(count - 1)]
        backward = [(target, source) for source, target in forward]
        low = lax.ppermute(
            lax.slice_in_dim(block, block.shape[dim] - width, None, axis=dim), axis, forward
        )
        high = lax.ppermute(lax.slice_in_dim(block, 0, width, axis=dim), axis, backward)
        block = jnp.concatenate([low, block, high], axis=dim)
    return block


def pool_pairs(values):
    height, width, depth = values.shape
    return jnp.max(values.reshape(height // 2, 2, width // 2, 2, depth), axis=(1, 3))


def contract_last(weight_rows, data):
    return lax.dot_general(
        weight_rows, data, (((1,), (1,)), ((), ())), preferred_element_type=jnp.float32
    )


def apply_norm(values, sums, squares, neck_width, gain_row, shift_row):
    floats = values.astype(jnp.float32)
    center = (sums / neck_width)[None, :]
    spread = (squares / neck_width)[None, :] - center * center
    scaled = (floats - center) * lax.rsqrt(spread + EPSILON)
    return (scaled * gain_row[:, None] + shift_row[:, None]).astype(jnp.bfloat16)


def cell_moments(values):
    floats = values.astype(jnp.float32)
    return (jnp.sum(floats, axis=0), jnp.sum(floats * floats, axis=0))


def conv_taps(totals, padded, weight, height, width):
    depth = padded.shape[0]
    for tap_index in range(9):
        row_off = tap_index // 3
        col_off = tap_index % 3
        window = padded[:, row_off : row_off + height, col_off : col_off + width].reshape(
            depth, height * width
        )
        rows_used = weight[:, tap_index, :]
        totals = totals + jnp.dot(rows_used, window, preferred_element_type=jnp.float32)
    return totals


def pyramid_level(lateral, height, width, level_index, output_conv, norm_gain, norm_shift):
    local_ch = lateral.shape[0]
    neck_width = local_ch * lax.axis_size("mp")
    own_first = lax.axis_index("mp") * local_ch
    weight = output_conv[level_index]
    initial = jnp.zeros((local_ch, height * width), jnp.float32)
    gathered = lax.all_gather(lateral, "mp", axis=0, tiled=True)
    sums, squares = cell_moments(gathered)
    normed = apply_norm(
        gathered, sums, squares, neck_width, norm_gain[2 * level_index], norm_shift[2 * level_index]
    )
    rimmed = extended(normed.reshape(neck_width, height, width), (("space", 1),), 1)
    padded = jnp.pad(rimmed, ((0, 0), (0, 0), (1, 1)))
    conv_out = conv_taps(initial, padded, weight, height, width)
    convolved = conv_out.astype(jnp.bfloat16)
    sums, squares = lax.psum(cell_moments(convolved), "mp")
    gain_row = lax.dynamic_slice_in_dim(norm_gain[2 * level_index + 1], own_first, local_ch, 0)
    shift_row = lax.dynamic_slice_in_dim(norm_shift[2 * level_index + 1], own_first, local_ch, 0)
    return apply_norm(convolved, sums, squares, neck_width, gain_row, shift_row)


def channel_pyramid(
    features,
    deconv_weight,
    deconv_bias,
    lateral_eight,
    lateral_coarse,
    output_conv,
    norm_gain,
    norm_shift,
):
    row_count, col_count, _ = features.shape
    half_local = deconv_weight.shape[1]
    neck_local = lateral_coarse.shape[1]
    pixels = row_count * col_count
    coarse_pixels = row_count // 2 * (col_count // 2)
    deconv_flat = deconv_weight.reshape(4 * half_local, deconv_weight.shape[2])
    piece = lax.all_gather(features, "mp", axis=2, tiled=True)
    depth = piece.shape[2]
    flattened = piece.reshape(pixels, depth)
    raised = contract_last(deconv_flat, flattened)
    middle = contract_last(lateral_coarse[0], flattened)
    pooled_flat = pool_pairs(piece).reshape(coarse_pixels, depth)
    coarse = contract_last(lateral_coarse[1], pooled_flat)
    raised, middle, coarse = (raised, middle, coarse)
    raised = (
        raised.reshape(2, 2, half_local, row_count, col_count)
        + deconv_bias[None, None, :, None, None]
    )
    upsampled = raised.transpose(2, 3, 0, 4, 1).reshape(half_local, 4 * pixels).astype(jnp.bfloat16)
    piece = lax.all_gather(upsampled, "mp", axis=0, tiled=True)
    lateral_sum = jnp.dot(lateral_eight, piece, preferred_element_type=jnp.float32)
    lat_eight = lateral_sum.astype(jnp.bfloat16)
    lat_sixteen = middle.astype(jnp.bfloat16)
    lat_thirty = coarse.astype(jnp.bfloat16)
    level_eight = pyramid_level(
        lat_eight, 2 * row_count, 2 * col_count, 0, output_conv, norm_gain, norm_shift
    )
    level_sixteen = pyramid_level(
        lat_sixteen, row_count, col_count, 1, output_conv, norm_gain, norm_shift
    )
    level_thirty = pyramid_level(
        lat_thirty, row_count // 2, col_count // 2, 2, output_conv, norm_gain, norm_shift
    )
    level_sixty = level_thirty.reshape(neck_local, row_count // 2, col_count // 2)[
        :, ::2, ::2
    ].reshape(neck_local, -1)
    return (level_eight, level_sixteen, level_thirty, level_sixty)


def nt(left, right):
    return lax.dot_general(
        left, right, (((1,), (1,)), ((), ())), preferred_element_type=jnp.float32
    )


def lane_norm(values, gain_row, shift_row):
    floats = values.astype(jnp.float32)
    center = jnp.mean(floats, axis=1, keepdims=True)
    spread = jnp.mean(floats * floats, axis=1, keepdims=True) - center * center
    scaled = (floats - center) * lax.rsqrt(spread + EPSILON)
    return scaled * gain_row + shift_row


def shifted(values, step, cols):
    count = values.shape[0]
    moved = pltpu.roll(values, step % count, 0)
    col = lax.rem(lax.broadcasted_iota(jnp.int32, values.shape, 0), cols)
    edge = 0 if step > 0 else cols - 1
    return jnp.where(col == edge, 0.0, moved)


RAISE, COARSE, MOMENT, FINAL = range(4)
KINDS = FINAL + 2


def pyramid_kernel(
    n, bands, rows, cols, neck, half,
    feat, dw, bias, lat, lc, oc, gain, shift,
    o8, o16, o32, o64,
    fbuf, dwv, lcv, latw, w0, w1, w2, acc, pool, ubuf, usend, cbuf, v8, x16, x32,
    halo8, halo16, halo32, send8, send16, send32, mbuf, inter, osend,
    ssem, rsem, lsem, hs, hr, fs, fr, ws, wr,
):
    me = lax.axis_index("mp")
    band = lax.axis_index("space")
    layer = lax.axis_index("dp")
    layers = lax.axis_size("dp")
    depth = feat.shape[1]
    own = neck // n
    hown = half // n
    px = rows * cols
    prows = rows // n
    part = prows * cols
    r2, c2 = rows // 2, cols // 2
    px2 = r2 * c2

    def at_mp(k):
        fast = lax.rem(lax.rem(me, 2) + k % 2, 2)
        slow = lax.rem(lax.div(me, 2) + k // 2, 2)
        return 2 * slow + fast

    locals_ = [
        pltpu.make_async_copy(feat, fbuf.at[0], lsem.at[0]),
        pltpu.make_async_copy(dw, dwv, lsem.at[1]),
        pltpu.make_async_copy(lc, lcv, lsem.at[2]),
        pltpu.make_async_copy(lat, latw.at[pl.ds(pl.multiple_of(me * own, own), own)], lsem.at[3]),
        pltpu.make_async_copy(oc.at[0], w0.at[:, pl.ds(pl.multiple_of(me * own, own), own)], lsem.at[4]),
        pltpu.make_async_copy(oc.at[1], w1, lsem.at[5]),
        pltpu.make_async_copy(oc.at[2], w2, lsem.at[6]),
    ]
    for copy in locals_:
        copy.start()

    barrier = pltpu.get_barrier_semaphore()
    for b in range(bands):
        for k in range(n):
            if b == 0 and k == 0:
                continue
            pl.semaphore_signal(
                barrier,
                inc=1,
                device_id={"space": lax.rem(band + b, bands), "mp": at_mp(k)},
                device_id_type=MESH,
            )
    for b in range(1, layers):
        pl.semaphore_signal(
            barrier, inc=1, device_id={"dp": lax.rem(layer + b, layers)}, device_id_type=MESH
        )
    pl.semaphore_wait(barrier, bands * n - 1 + layers - 1)

    def remote(src, dst, kind, k):
        return pltpu.make_async_remote_copy(
            src_ref=src,
            dst_ref=dst,
            send_sem=ssem.at[kind, k],
            recv_sem=rsem.at[kind, k],
            device_id={"mp": at_mp(k)},
            device_id_type=MESH,
        )

    peers = list(range(1, n))
    mine = pl.ds(pl.multiple_of(me * own, own), own)
    sends = {}

    def launch(kind, make):
        for k in peers:
            copy = remote(*make(k), kind, k)
            copy.start()
            sends[kind, k] = copy

    top = pl.ds(0, px // 2)
    low = pl.ds(px // 2, px // 2)

    def feature_copy(src, dst, slot, half_at, k):
        return pltpu.make_async_remote_copy(
            src_ref=src, dst_ref=dst, send_sem=fs.at[slot, half_at],
            recv_sem=fr.at[slot, half_at], device_id={"mp": at_mp(k)}, device_id_type=MESH)

    first = {}
    for k, half_at in ((1, 0), (2, 1), (1, 1), (2, 0)):
        span = (top, low)[half_at]
        first[k, half_at] = feature_copy(feat.at[span], fbuf.at[k, span], k, half_at, k)
    first[1, 0].start()
    first[2, 1].start()

    piece = own // layers
    taps = oc.shape[1]
    widths = (neck // bands, half // bands)

    def block(which, src, rows_at, count, ref, own_ref):
        lanes = pl.ds(pl.multiple_of(band * widths[which], widths[which]), widths[which])
        base = rows_at if own_ref else src * own + rows_at
        span = pl.ds(pl.multiple_of(base, count), count)
        if which == 0:
            return ref.at[0, :, span, lanes] if own_ref else ref.at[:, span, lanes]
        return ref.at[span, lanes]

    sources = (oc, lat)
    targets = (w0, latw)
    weight_sends = []
    stage_one, stage_two, stage_three = {}, {}, {}
    start_rows = layer * piece
    for which in (1, 0):
        for k in range(1, n):
            copy = pltpu.make_async_remote_copy(
                src_ref=block(which, me, start_rows, piece, sources[which], True),
                dst_ref=block(which, me, start_rows, piece, targets[which], False),
                send_sem=ws.at[which, 0, k], recv_sem=wr.at[which, 0, k],
                device_id={"mp": at_mp(k)}, device_id_type=MESH)
            copy.start()
            stage_one[which, k] = copy
    first[1, 1].start()
    first[2, 0].start()

    def share_along_dp():
        for which in (1, 0):
            for k in range(1, n):
                stage_one[which, k].wait_recv()
                for step in range(1, layers):
                    here = block(which, at_mp(k), start_rows, piece, targets[which], False)
                    copy = pltpu.make_async_remote_copy(
                        src_ref=here, dst_ref=here,
                        send_sem=ws.at[which, step, k], recv_sem=wr.at[which, step, k],
                        device_id={"dp": lax.rem(layer + step, layers)}, device_id_type=MESH)
                    copy.start()
                    stage_two[which, k, step] = copy

    def share_with_core(which):
        for k in range(1, n):
            for step in range(1, layers):
                stage_two[which, k, step].wait_recv()
            here = block(which, at_mp(k), 0, own, targets[which], False)
            copy = pltpu.make_async_remote_copy(
                src_ref=here, dst_ref=here,
                send_sem=ws.at[which, layers, k], recv_sem=wr.at[which, layers, k],
                device_id={"space": lax.rem(band + 1, bands)}, device_id_type=MESH)
            copy.start()
            stage_three[which, k] = copy

    lat16 = jnp.zeros((own, px), jnp.float32)
    lat32 = jnp.zeros((own, px2), jnp.float32)
    for k in range(n):
        if k == 0:
            for i in range(3):
                locals_[i].wait()
        elif k == 1:
            first[1, 0].wait_recv()
            relay = [feature_copy(fbuf.at[1, top], fbuf.at[3, top], 3, 0, 2)]
            relay[0].start()
            first[2, 1].wait_recv()
            relay.append(feature_copy(fbuf.at[2, low], fbuf.at[3, low], 3, 1, 1))
            relay[1].start()
            first[1, 1].wait_recv()
        elif k == 2:
            first[2, 0].wait_recv()
        else:
            share_along_dp()
            relay[0].wait_recv()
            relay[1].wait_recv()
        src = at_mp(k)
        span = pl.ds(pl.multiple_of(src * depth, depth), depth)
        values = fbuf[k]
        term = nt(values, dwv[:, span])
        if k == 0:
            acc[...] = term
        else:
            acc[...] += term
        lat16 = lat16 + nt(lcv[0:own, span], values)
        floats = values.astype(jnp.float32).reshape(r2, 2 * cols, depth)
        tall = jnp.maximum(floats[:, :cols], floats[:, cols:]).reshape(r2 * cols, depth)
        halves = []
        for g in range(depth // 128):
            pool[...] = tall[:, g * 128 : (g + 1) * 128]
            halves.append(jnp.maximum(pool[pl.ds(0, px2, stride=2), :], pool[pl.ds(1, px2, stride=2), :]))
        pooled = jnp.concatenate(halves, axis=1).astype(jnp.bfloat16)
        lat32 = lat32 + nt(lcv[own:, span], pooled)

    for d in range(n):
        for il in range(prows):
            base = (d * prows + il) * cols
            for a in range(2):
                for b in range(2):
                    tap = 2 * a + b
                    value = acc[base : base + cols, tap * hown : (tap + 1) * hown] + bias[...]
                    at = (b * 2 * prows + 2 * il + a) * cols
                    usend[d, at : at + cols, :] = value.astype(jnp.bfloat16)
    launch(RAISE, lambda k: (usend.at[at_mp(k)], ubuf.at[k]))
    cbuf[mine, 0:px] = lat16.astype(jnp.bfloat16)
    cbuf[mine, px:] = lat32.astype(jnp.bfloat16)
    launch(COARSE, lambda k: (cbuf.at[mine], cbuf.at[mine]))
    share_with_core(1)

    locals_[3].wait()
    for k in peers:
        stage_three[1, k].wait_recv()
    total = nt(usend[me], latw[:, pl.ds(pl.multiple_of(me * hown, hown), hown)])
    for k in peers:
        sends[RAISE, k].wait_recv()
        src = at_mp(k)
        total = total + nt(ubuf[k], latw[:, pl.ds(pl.multiple_of(src * hown, hown), hown)])
    own_rows = 2 * prows
    wide = own_rows * cols
    normed = lane_norm(total.astype(jnp.bfloat16), gain[0:1, :], shift[0:1, :])
    rounded = normed.astype(jnp.bfloat16)
    for b in range(2):
        send8[0, b * cols : (b + 1) * cols, :] = rounded[b * wide : b * wide + cols]
        send8[1, b * cols : (b + 1) * cols, :] = rounded[(b + 1) * wide - cols : (b + 1) * wide]

    place = band * n + me
    last = bands * n - 1

    def halo(src_buf, dst_buf, level, low_if, low_dev, high_if, high_dev):
        low = pltpu.make_async_remote_copy(
            src_ref=src_buf.at[0], dst_ref=dst_buf.at[1], send_sem=hs.at[level, 0],
            recv_sem=hr.at[level, 1], device_id=low_dev, device_id_type=MESH)
        high = pltpu.make_async_remote_copy(
            src_ref=src_buf.at[1], dst_ref=dst_buf.at[0], send_sem=hs.at[level, 1],
            recv_sem=hr.at[level, 0], device_id=high_dev, device_id_type=MESH)

        @pl.when(low_if)
        def _():
            low.start()

        @pl.when(high_if)
        def _():
            high.start()

        def finish():
            @pl.when(low_if)
            def _():
                low.wait_send()
                high_like = pltpu.make_async_remote_copy(
                    src_ref=src_buf.at[1], dst_ref=dst_buf.at[0], send_sem=hs.at[level, 1],
                    recv_sem=hr.at[level, 0], device_id=low_dev, device_id_type=MESH)
                high_like.wait_recv()

            @pl.when(high_if)
            def _():
                high.wait_send()
                low_like = pltpu.make_async_remote_copy(
                    src_ref=src_buf.at[0], dst_ref=dst_buf.at[1], send_sem=hs.at[level, 0],
                    recv_sem=hr.at[level, 1], device_id=high_dev, device_id_type=MESH)
                low_like.wait_recv()

            @pl.when(jnp.logical_not(low_if))
            def _():
                dst_buf[0] = jnp.zeros(dst_buf.shape[1:], dst_buf.dtype)

            @pl.when(jnp.logical_not(high_if))
            def _():
                dst_buf[1] = jnp.zeros(dst_buf.shape[1:], dst_buf.dtype)

        return finish

    def device_of(index):
        return {"space": lax.div(index, n), "mp": lax.rem(index, n)}

    finish8 = halo(
        send8, halo8, 0,
        place > 0, device_of(jnp.maximum(place - 1, 0)),
        place < last, device_of(jnp.minimum(place + 1, last)),
    )
    zero = normed[0:wide]
    one = normed[wide:]

    def fill8(at, count, even, odd):
        v8[0, at : at + count, :] = shifted(odd, 1, cols).astype(jnp.bfloat16)
        v8[1, at : at + count, :] = even.astype(jnp.bfloat16)
        v8[2, at : at + count, :] = odd.astype(jnp.bfloat16)
        v8[3, at : at + count, :] = shifted(even, -1, cols).astype(jnp.bfloat16)

    fill8(cols, wide, zero, one)

    share_with_core(0)
    for k in peers:
        sends[COARSE, k].wait_recv()
    coarse = cbuf[...].astype(jnp.float32).T
    levels = (
        (1, rows, cols, x16, send16, halo16, w1, coarse[:px], 0),
        (2, r2, c2, x32, send32, halo32, w2, coarse[px:], px),
    )

    def fill(x, at, count, values, width):
        x[0, at : at + count, :] = shifted(values, 1, width).astype(jnp.bfloat16)
        x[1, at : at + count, :] = values.astype(jnp.bfloat16)
        x[2, at : at + count, :] = shifted(values, -1, width).astype(jnp.bfloat16)

    finishes = []
    for level, height, width, x, snd, hal, w, values, at in levels:
        out = lane_norm(values, gain[2 * level : 2 * level + 1, :], shift[2 * level : 2 * level + 1, :])
        fill(x, width, height * width, out, width)
        snd[0] = out[:width].astype(jnp.bfloat16)
        snd[1] = out[height * width - width :].astype(jnp.bfloat16)
        finishes.append(halo(
            snd, hal, level,
            band > 0, {"space": jnp.maximum(band - 1, 0)},
            band < bands - 1, {"space": jnp.minimum(band + 1, bands - 1)},
        ))
    finish8()
    fill8(0, cols, halo8[0, 0:cols].astype(jnp.float32), halo8[0, cols:].astype(jnp.float32))
    fill8(cols + wide, cols, halo8[1, 0:cols].astype(jnp.float32), halo8[1, cols:].astype(jnp.float32))
    locals_[4].wait()
    for k in peers:
        stage_three[0, k].wait_recv()
    part_px = wide // 2
    for part_at in range(2):
        result = jnp.zeros((2 * part_px, neck), jnp.float32)
        for tap in range(9):
            r, q = tap // 3, tap % 3
            at = r * cols + part_at * part_px
            window = v8[q : q + 2, at : at + part_px, :].reshape(2 * part_px, neck)
            result = result + nt(window, w0[tap])
        out = lane_norm(result.astype(jnp.bfloat16), gain[1:2, :], shift[1:2, :])
        for g in range(neck // 128):
            for b in range(2):
                inter[g, pl.ds(2 * part_at * part_px + b, part_px, stride=2), :] = out[
                    b * part_px : (b + 1) * part_px, g * 128 : (g + 1) * 128
                ]
        for g in range(neck // 128):
            osend[part_at, g * 128 : (g + 1) * 128, :] = inter[
                g, part_at * wide : (part_at + 1) * wide, :
            ].T.astype(jnp.bfloat16)
        cells = pl.ds(pl.multiple_of((2 * me + part_at) * wide, wide), wide)
        launch(
            FINAL + part_at,
            lambda k: (
                osend.at[part_at, pl.ds(pl.multiple_of(at_mp(k) * own, own), own)],
                o8.at[:, cells],
            ),
        )
        o8[:, cells] = osend[part_at, mine, :]

    maps = []
    locals_[5].wait()
    locals_[6].wait()
    for (level, height, width, x, snd, hal, w, values, at), done in zip(levels, finishes):
        done()
        fill(x, 0, width, hal[0].astype(jnp.float32), width)
        fill(x, (height + 1) * width, width, hal[1].astype(jnp.float32), width)
        result = jnp.zeros((own, height * width), jnp.float32)
        for tap in range(9):
            r, q = tap // 3, tap % 3
            result = result + nt(
                w[tap], x[q, r * width : (r + height) * width, :]
            )
        result = result.astype(jnp.bfloat16).astype(jnp.float32)
        span = slice(at, at + height * width)
        mbuf[0, 0:1, span] = jnp.sum(result, axis=0, keepdims=True)
        mbuf[0, 1:2, span] = jnp.sum(result * result, axis=0, keepdims=True)
        maps.append(result)
    launch(MOMENT, lambda k: (mbuf.at[0], mbuf.at[k]))

    lane = lax.broadcasted_iota(jnp.int32, (own, neck), 1)
    row = lax.broadcasted_iota(jnp.int32, (own, neck), 0)
    chosen = lane == row + me * own

    def own_column(table, index):
        return jnp.sum(
            jnp.where(chosen, table[index : index + 1, :], 0.0), axis=1, keepdims=True
        )

    for k in peers:
        sends[MOMENT, k].wait_recv()
    moments = mbuf[0]
    for k in peers:
        moments = moments + mbuf[k]
    moments = moments / neck
    for (level, height, width, x, snd, hal, w, values, at), result in zip(levels, maps):
        span = slice(at, at + height * width)
        center = moments[0:1, span]
        spread = moments[1:2, span] - center * center
        scaled = (result - center) * lax.rsqrt(spread + EPSILON)
        final = (
            scaled * own_column(gain, 2 * level + 1) + own_column(shift, 2 * level + 1)
        ).astype(jnp.bfloat16)
        if level == 1:
            o16[...] = final
        else:
            o32[...] = final
            count = o64.shape[0]
            wide2 = c2 // 2
            cell = lax.broadcasted_iota(jnp.int32, (count, px2), 1)
            target = lax.broadcasted_iota(jnp.int32, (count, px2), 0)
            wanted = lax.div(target, wide2) * (2 * c2) + 2 * lax.rem(target, wide2)
            pick = jnp.where(cell == wanted, 1.0, 0.0).astype(jnp.bfloat16)
            o64[...] = nt(pick, final).astype(jnp.bfloat16)

    for copy in (*first.values(), *relay, *stage_one.values(), *stage_two.values(), *stage_three.values()):
        copy.wait_send()
    for kind in range(KINDS):
        for k in peers:
            sends[kind, k].wait_send()
    for k in peers:
        sends[FINAL, k].wait_recv()
        sends[FINAL + 1, k].wait_recv()


def hand_over(*refs):
    count = len(refs) // 2
    for source, target in zip(refs[:count], refs[count:]):
        target[...] = source[...]


def fused(features, deconv_weight, deconv_bias, lateral_eight, lateral_coarse, output_conv,
          norm_gain, norm_shift):
    n = lax.axis_size("mp")
    bands = lax.axis_size("space")
    rows, cols, depth = features.shape
    full = deconv_weight.shape[2]
    hown = deconv_weight.shape[1]
    own = lateral_eight.shape[0]
    neck, half = own * n, hown * n
    layers = lax.axis_size("dp")
    px, px2 = rows * cols, rows * cols // 4
    wide = 2 * (rows // n) * cols
    bf, f32 = jnp.bfloat16, jnp.float32
    vmem = pl.BlockSpec(memory_space=pltpu.VMEM)
    hbm = pl.BlockSpec(memory_space=pl.ANY)
    shapes = [
        ((n, px, depth), bf), ((4 * hown, full), bf), ((2 * own, full), bf),
        ((neck, half), bf), ((9, neck, neck), bf), ((9, own, neck), bf), ((9, own, neck), bf),
        ((px, 4 * hown), f32), ((px // 2, 128), f32), ((n, 2 * wide, hown), bf),
        ((n, 2 * wide, hown), bf), ((neck, px + px2), bf),
        ((4, wide + 2 * cols, neck), bf), ((3, px + 2 * cols, neck), bf),
        ((3, px2 + cols, neck), bf),
        ((2, 2 * cols, neck), bf), ((2, cols, neck), bf), ((2, cols // 2, neck), bf),
        ((2, 2 * cols, neck), bf), ((2, cols, neck), bf), ((2, cols // 2, neck), bf),
        ((n, 8, px + px2), f32), ((neck // 128, 2 * wide, 128), f32), ((2, neck, wide), bf),
    ]
    results = pl.pallas_call(
        functools.partial(pyramid_kernel, n, bands, rows, cols, neck, half),
        out_shape=[
            jax.ShapeDtypeStruct((own, 4 * px), bf), jax.ShapeDtypeStruct((own, px), bf),
            jax.ShapeDtypeStruct((own, px2), bf), jax.ShapeDtypeStruct((px2 // 4, own), bf),
        ],
        in_specs=[hbm, hbm, vmem, hbm, hbm, hbm, vmem, vmem],
        out_specs=[vmem] * 4,
        scratch_shapes=[pltpu.VMEM(s, d) for s, d in shapes] + [
            pltpu.SemaphoreType.DMA((KINDS, n)), pltpu.SemaphoreType.DMA((KINDS, n)),
            pltpu.SemaphoreType.DMA((7,)), pltpu.SemaphoreType.DMA((3, 2)),
            pltpu.SemaphoreType.DMA((3, 2)),
            pltpu.SemaphoreType.DMA((n, 2)), pltpu.SemaphoreType.DMA((n, 2)),
            pltpu.SemaphoreType.DMA((2, layers + 1, n)), pltpu.SemaphoreType.DMA((2, layers + 1, n)),
        ],
        compiler_params=pltpu.CompilerParams(
            collective_id=0, has_side_effects=True, vmem_limit_bytes=56 << 20
        ),
    )(
        features.reshape(px, depth), deconv_weight.reshape(4 * hown, full),
        deconv_bias.reshape(1, hown), lateral_eight, lateral_coarse.reshape(2 * own, full),
        output_conv.transpose(0, 2, 1, 3), norm_gain, norm_shift,
    )
    eight, sixteen, thirty, sixty = pl.pallas_call(
        hand_over,
        out_shape=[jax.ShapeDtypeStruct(r.shape, r.dtype) for r in results],
        in_specs=[vmem] * 4,
        out_specs=[vmem] * 4,
    )(*results)
    return eight, sixteen, thirty, sixty.T


def per_device(features, deconv_weight, *rest):
    n = lax.axis_size("mp")
    rows, cols, depth = features.shape
    aligned = depth % 128 == 0 and deconv_weight.shape[1] % 128 == 0
    bands, layers = lax.axis_size("space"), lax.axis_size("dp")
    own, neck = rest[1].shape[0], rest[3].shape[3]
    aligned = aligned and n == 4 and bands == 2 and own % (16 * layers) == 0 and neck % (128 * bands) == 0
    if aligned and rows % n == 0 and rows % 4 == 0 and cols % 64 == 0:
        return tuple(fused(features, deconv_weight, *rest))
    return channel_pyramid(features, deconv_weight, *rest)


def solution(mesh):
    return jax.shard_map(
        per_device,
        mesh=mesh,
        in_specs=(
            P(("dp", "space"), None, "mp"),
            P(None, "mp", None),
            P("mp"),
            P("mp", None),
            P(None, "mp", None),
            P(None, "mp", None, None),
            P(),
            P(),
        ),
        out_specs=(
            P("mp", ("dp", "space")),
            P("mp", ("dp", "space")),
            P("mp", ("dp", "space")),
            P("mp", ("dp", "space")),
        ),
        check_vma=False,
    )
```

```python
import functools

import jax
import jax.numpy as jnp
from jax import lax
from jax.experimental import pallas as pl
from jax.experimental.pallas import tpu as pltpu
from jax.sharding import PartitionSpec as P

EPSILON = 1e-06
MESH = pl.DeviceIdType.MESH


def extended(block, sides, width):
    for axis, dim in sides:
        count = lax.axis_size(axis)
        forward = [(i, i + 1) for i in range(count - 1)]
        backward = [(target, source) for source, target in forward]
        low = lax.ppermute(
            lax.slice_in_dim(block, block.shape[dim] - width, None, axis=dim), axis, forward
        )
        high = lax.ppermute(lax.slice_in_dim(block, 0, width, axis=dim), axis, backward)
        block = jnp.concatenate([low, block, high], axis=dim)
    return block


def pool_pairs(values):
    height, width, depth = values.shape
    return jnp.max(values.reshape(height // 2, 2, width // 2, 2, depth), axis=(1, 3))


def contract_last(weight_rows, data):
    return lax.dot_general(
        weight_rows, data, (((1,), (1,)), ((), ())), preferred_element_type=jnp.float32
    )


def apply_norm(values, sums, squares, neck_width, gain_row, shift_row):
    floats = values.astype(jnp.float32)
    center = (sums / neck_width)[None, :]
    spread = (squares / neck_width)[None, :] - center * center
    scaled = (floats - center) * lax.rsqrt(spread + EPSILON)
    return (scaled * gain_row[:, None] + shift_row[:, None]).astype(jnp.bfloat16)


def cell_moments(values):
    floats = values.astype(jnp.float32)
    return (jnp.sum(floats, axis=0), jnp.sum(floats * floats, axis=0))


def conv_taps(totals, padded, weight, height, width):
    depth = padded.shape[0]
    for tap_index in range(9):
        row_off = tap_index // 3
        col_off = tap_index % 3
        window = padded[:, row_off : row_off + height, col_off : col_off + width].reshape(
            depth, height * width
        )
        rows_used = weight[:, tap_index, :]
        totals = totals + jnp.dot(rows_used, window, preferred_element_type=jnp.float32)
    return totals


def pyramid_level(lateral, height, width, level_index, output_conv, norm_gain, norm_shift):
    local_ch = lateral.shape[0]
    neck_width = local_ch * lax.axis_size("mp")
    own_first = lax.axis_index("mp") * local_ch
    weight = output_conv[level_index]
    initial = jnp.zeros((local_ch, height * width), jnp.float32)
    gathered = lax.all_gather(lateral, "mp", axis=0, tiled=True)
    sums, squares = cell_moments(gathered)
    normed = apply_norm(
        gathered, sums, squares, neck_width, norm_gain[2 * level_index], norm_shift[2 * level_index]
    )
    rimmed = extended(normed.reshape(neck_width, height, width), (("space", 1),), 1)
    padded = jnp.pad(rimmed, ((0, 0), (0, 0), (1, 1)))
    conv_out = conv_taps(initial, padded, weight, height, width)
    convolved = conv_out.astype(jnp.bfloat16)
    sums, squares = lax.psum(cell_moments(convolved), "mp")
    gain_row = lax.dynamic_slice_in_dim(norm_gain[2 * level_index + 1], own_first, local_ch, 0)
    shift_row = lax.dynamic_slice_in_dim(norm_shift[2 * level_index + 1], own_first, local_ch, 0)
    return apply_norm(convolved, sums, squares, neck_width, gain_row, shift_row)


def channel_pyramid(
    features,
    deconv_weight,
    deconv_bias,
    lateral_eight,
    lateral_coarse,
    output_conv,
    norm_gain,
    norm_shift,
):
    row_count, col_count, _ = features.shape
    half_local = deconv_weight.shape[1]
    neck_local = lateral_coarse.shape[1]
    pixels = row_count * col_count
    coarse_pixels = row_count // 2 * (col_count // 2)
    deconv_flat = deconv_weight.reshape(4 * half_local, deconv_weight.shape[2])
    piece = lax.all_gather(features, "mp", axis=2, tiled=True)
    depth = piece.shape[2]
    flattened = piece.reshape(pixels, depth)
    raised = contract_last(deconv_flat, flattened)
    middle = contract_last(lateral_coarse[0], flattened)
    pooled_flat = pool_pairs(piece).reshape(coarse_pixels, depth)
    coarse = contract_last(lateral_coarse[1], pooled_flat)
    raised, middle, coarse = (raised, middle, coarse)
    raised = (
        raised.reshape(2, 2, half_local, row_count, col_count)
        + deconv_bias[None, None, :, None, None]
    )
    upsampled = raised.transpose(2, 3, 0, 4, 1).reshape(half_local, 4 * pixels).astype(jnp.bfloat16)
    piece = lax.all_gather(upsampled, "mp", axis=0, tiled=True)
    lateral_sum = jnp.dot(lateral_eight, piece, preferred_element_type=jnp.float32)
    lat_eight = lateral_sum.astype(jnp.bfloat16)
    lat_sixteen = middle.astype(jnp.bfloat16)
    lat_thirty = coarse.astype(jnp.bfloat16)
    level_eight = pyramid_level(
        lat_eight, 2 * row_count, 2 * col_count, 0, output_conv, norm_gain, norm_shift
    )
    level_sixteen = pyramid_level(
        lat_sixteen, row_count, col_count, 1, output_conv, norm_gain, norm_shift
    )
    level_thirty = pyramid_level(
        lat_thirty, row_count // 2, col_count // 2, 2, output_conv, norm_gain, norm_shift
    )
    level_sixty = level_thirty.reshape(neck_local, row_count // 2, col_count // 2)[
        :, ::2, ::2
    ].reshape(neck_local, -1)
    return (level_eight, level_sixteen, level_thirty, level_sixty)


def nt(left, right):
    return lax.dot_general(
        left, right, (((1,), (1,)), ((), ())), preferred_element_type=jnp.float32
    )


def lane_norm(values, gain_row, shift_row):
    floats = values.astype(jnp.float32)
    center = jnp.mean(floats, axis=1, keepdims=True)
    spread = jnp.mean(floats * floats, axis=1, keepdims=True) - center * center
    scaled = (floats - center) * lax.rsqrt(spread + EPSILON)
    return scaled * gain_row + shift_row


def shifted(values, step, cols):
    count = values.shape[0]
    moved = pltpu.roll(values, step % count, 0)
    col = lax.rem(lax.broadcasted_iota(jnp.int32, values.shape, 0), cols)
    edge = 0 if step > 0 else cols - 1
    return jnp.where(col == edge, 0.0, moved)


RAISE, COARSE, MOMENT, FINAL = range(4)
KINDS = FINAL + 2


def pyramid_kernel(
    n, bands, rows, cols, neck, half,
    feat, dw, bias, lat, lc, oc, gain, shift,
    o8, o16, o32, o64,
    fbuf, dwv, lcv, latw, w0, w1, w2, acc, pool, ubuf, usend, cbuf, v8, x16, x32,
    halo8, halo16, halo32, send8, send16, send32, mbuf, inter, osend,
    ssem, rsem, lsem, hs, hr, fs, fr, ws, wr,
):
    me = lax.axis_index("mp")
    band = lax.axis_index("space")
    layer = lax.axis_index("dp")
    layers = lax.axis_size("dp")
    depth = feat.shape[1]
    own = neck // n
    hown = half // n
    px = rows * cols
    prows = rows // n
    part = prows * cols
    r2, c2 = rows // 2, cols // 2
    px2 = r2 * c2

    def at_mp(k):
        fast = lax.rem(lax.rem(me, 2) + k % 2, 2)
        slow = lax.rem(lax.div(me, 2) + k // 2, 2)
        return 2 * slow + fast

    locals_ = [
        pltpu.make_async_copy(feat, fbuf.at[0], lsem.at[0]),
        pltpu.make_async_copy(dw, dwv, lsem.at[1]),
        pltpu.make_async_copy(lc, lcv, lsem.at[2]),
        pltpu.make_async_copy(lat, latw.at[pl.ds(pl.multiple_of(me * own, own), own)], lsem.at[3]),
        pltpu.make_async_copy(oc.at[0], w0.at[:, pl.ds(pl.multiple_of(me * own, own), own)], lsem.at[4]),
        pltpu.make_async_copy(oc.at[1], w1, lsem.at[5]),
        pltpu.make_async_copy(oc.at[2], w2, lsem.at[6]),
    ]
    for copy in locals_:
        copy.start()

    barrier = pltpu.get_barrier_semaphore()
    for b in range(bands):
        for k in range(n):
            if b == 0 and k == 0:
                continue
            pl.semaphore_signal(
                barrier,
                inc=1,
                device_id={"space": lax.rem(band + b, bands), "mp": at_mp(k)},
                device_id_type=MESH,
            )
    for b in range(1, layers):
        pl.semaphore_signal(
            barrier, inc=1, device_id={"dp": lax.rem(layer + b, layers)}, device_id_type=MESH
        )
    pl.semaphore_wait(barrier, bands * n - 1 + layers - 1)

    def remote(src, dst, kind, k):
        return pltpu.make_async_remote_copy(
            src_ref=src,
            dst_ref=dst,
            send_sem=ssem.at[kind, k],
            recv_sem=rsem.at[kind, k],
            device_id={"mp": at_mp(k)},
            device_id_type=MESH,
        )

    peers = list(range(1, n))
    mine = pl.ds(pl.multiple_of(me * own, own), own)
    sends = {}

    def launch(kind, make):
        for k in peers:
            copy = remote(*make(k), kind, k)
            copy.start()
            sends[kind, k] = copy

    top = pl.ds(0, px // 2)
    low = pl.ds(px // 2, px // 2)

    def feature_copy(src, dst, slot, half_at, k):
        return pltpu.make_async_remote_copy(
            src_ref=src, dst_ref=dst, send_sem=fs.at[slot, half_at],
            recv_sem=fr.at[slot, half_at], device_id={"mp": at_mp(k)}, device_id_type=MESH)

    first = {}
    for k, half_at in ((1, 0), (2, 1), (1, 1), (2, 0)):
        span = (top, low)[half_at]
        first[k, half_at] = feature_copy(feat.at[span], fbuf.at[k, span], k, half_at, k)
    first[1, 0].start()
    first[2, 1].start()

    piece = own // layers
    taps = oc.shape[1]
    widths = (neck // bands, half // bands)

    def block(which, src, rows_at, count, ref, own_ref):
        lanes = pl.ds(pl.multiple_of(band * widths[which], widths[which]), widths[which])
        base = rows_at if own_ref else src * own + rows_at
        span = pl.ds(pl.multiple_of(base, count), count)
        if which == 0:
            return ref.at[0, :, span, lanes] if own_ref else ref.at[:, span, lanes]
        return ref.at[span, lanes]

    sources = (oc, lat)
    targets = (w0, latw)
    weight_sends = []
    stage_one, stage_two, stage_three = {}, {}, {}
    start_rows = layer * piece
    for which in (1, 0):
        for k in range(1, n):
            copy = pltpu.make_async_remote_copy(
                src_ref=block(which, me, start_rows, piece, sources[which], True),
                dst_ref=block(which, me, start_rows, piece, targets[which], False),
                send_sem=ws.at[which, 0, k], recv_sem=wr.at[which, 0, k],
                device_id={"mp": at_mp(k)}, device_id_type=MESH)
            copy.start()
            stage_one[which, k] = copy
    first[1, 1].start()
    first[2, 0].start()

    def share_along_dp():
        for which in (1, 0):
            for k in range(1, n):
                stage_one[which, k].wait_recv()
                for step in range(1, layers):
                    here = block(which, at_mp(k), start_rows, piece, targets[which], False)
                    copy = pltpu.make_async_remote_copy(
                        src_ref=here, dst_ref=here,
                        send_sem=ws.at[which, step, k], recv_sem=wr.at[which, step, k],
                        device_id={"dp": lax.rem(layer + step, layers)}, device_id_type=MESH)
                    copy.start()
                    stage_two[which, k, step] = copy

    def share_with_core(which):
        for k in range(1, n):
            for step in range(1, layers):
                stage_two[which, k, step].wait_recv()
            here = block(which, at_mp(k), 0, own, targets[which], False)
            copy = pltpu.make_async_remote_copy(
                src_ref=here, dst_ref=here,
                send_sem=ws.at[which, layers, k], recv_sem=wr.at[which, layers, k],
                device_id={"space": lax.rem(band + 1, bands)}, device_id_type=MESH)
            copy.start()
            stage_three[which, k] = copy

    lat16 = jnp.zeros((own, px), jnp.float32)
    lat32 = jnp.zeros((own, px2), jnp.float32)

    def span_of(k):
        return pl.ds(pl.multiple_of(at_mp(k) * depth, depth), depth)

    def laterals(k, sixteen, thirty):
        span = span_of(k)
        values = fbuf[k]
        floats = values.astype(jnp.float32).reshape(r2, 2 * cols, depth)
        tall = jnp.maximum(floats[:, :cols], floats[:, cols:]).reshape(r2 * cols, depth)
        halves = []
        for g in range(depth // 128):
            pool[...] = tall[:, g * 128 : (g + 1) * 128]
            halves.append(
                jnp.maximum(pool[pl.ds(0, px2, stride=2), :], pool[pl.ds(1, px2, stride=2), :])
            )
        pooled = jnp.concatenate(halves, axis=1).astype(jnp.bfloat16)
        return sixteen + nt(lcv[0:own, span], values), thirty + nt(lcv[own:, span], pooled)

    for k in range(n):
        if k == 0:
            for i in range(3):
                locals_[i].wait()
        elif k == 1:
            first[1, 0].wait_recv()
            relay = [feature_copy(fbuf.at[1, top], fbuf.at[3, top], 3, 0, 2)]
            relay[0].start()
            first[2, 1].wait_recv()
            relay.append(feature_copy(fbuf.at[2, low], fbuf.at[3, low], 3, 1, 1))
            relay[1].start()
            share_along_dp()
            first[1, 1].wait_recv()
        elif k == 2:
            first[2, 0].wait_recv()
        else:
            relay[0].wait_recv()
            relay[1].wait_recv()
        if k == n - 1:
            break
        if k == 0:
            acc[...] = nt(fbuf[k], dwv[:, span_of(k)])
        else:
            acc[...] += nt(fbuf[k], dwv[:, span_of(k)])
        lat16, lat32 = laterals(k, lat16, lat32)

    for k in (3, 1, 2, 0):
        rows_at = pl.ds(pl.multiple_of(at_mp(k) * part, part), part)
        raised = acc[rows_at, :] + nt(fbuf[n - 1, rows_at, :], dwv[:, span_of(n - 1)])
        for il in range(prows):
            for a in range(2):
                for b in range(2):
                    tap = 2 * a + b
                    value = raised[
                        il * cols : (il + 1) * cols, tap * hown : (tap + 1) * hown
                    ] + bias[...]
                    at = (b * 2 * prows + 2 * il + a) * cols
                    usend[k, at : at + cols, :] = value.astype(jnp.bfloat16)
        if k > 0:
            copy = remote(usend.at[k], ubuf.at[k], RAISE, k)
            copy.start()
            sends[RAISE, k] = copy
    lat16, lat32 = laterals(n - 1, lat16, lat32)
    cbuf[mine, 0:px] = lat16.astype(jnp.bfloat16)
    cbuf[mine, px:] = lat32.astype(jnp.bfloat16)
    launch(COARSE, lambda k: (cbuf.at[mine], cbuf.at[mine]))
    share_with_core(1)

    locals_[3].wait()
    for k in peers:
        stage_three[1, k].wait_recv()
    total = nt(usend[0], latw[:, pl.ds(pl.multiple_of(me * hown, hown), hown)])
    for k in peers:
        sends[RAISE, k].wait_recv()
        src = at_mp(k)
        total = total + nt(ubuf[k], latw[:, pl.ds(pl.multiple_of(src * hown, hown), hown)])
    own_rows = 2 * prows
    wide = own_rows * cols
    normed = lane_norm(total.astype(jnp.bfloat16), gain[0:1, :], shift[0:1, :])
    rounded = normed.astype(jnp.bfloat16)
    for b in range(2):
        send8[0, b * cols : (b + 1) * cols, :] = rounded[b * wide : b * wide + cols]
        send8[1, b * cols : (b + 1) * cols, :] = rounded[(b + 1) * wide - cols : (b + 1) * wide]

    place = band * n + me
    last = bands * n - 1

    def halo(src_buf, dst_buf, level, low_if, low_dev, high_if, high_dev):
        low = pltpu.make_async_remote_copy(
            src_ref=src_buf.at[0], dst_ref=dst_buf.at[1], send_sem=hs.at[level, 0],
            recv_sem=hr.at[level, 1], device_id=low_dev, device_id_type=MESH)
        high = pltpu.make_async_remote_copy(
            src_ref=src_buf.at[1], dst_ref=dst_buf.at[0], send_sem=hs.at[level, 1],
            recv_sem=hr.at[level, 0], device_id=high_dev, device_id_type=MESH)

        @pl.when(low_if)
        def _():
            low.start()

        @pl.when(high_if)
        def _():
            high.start()

        def finish():
            @pl.when(low_if)
            def _():
                low.wait_send()
                high_like = pltpu.make_async_remote_copy(
                    src_ref=src_buf.at[1], dst_ref=dst_buf.at[0], send_sem=hs.at[level, 1],
                    recv_sem=hr.at[level, 0], device_id=low_dev, device_id_type=MESH)
                high_like.wait_recv()

            @pl.when(high_if)
            def _():
                high.wait_send()
                low_like = pltpu.make_async_remote_copy(
                    src_ref=src_buf.at[0], dst_ref=dst_buf.at[1], send_sem=hs.at[level, 0],
                    recv_sem=hr.at[level, 1], device_id=high_dev, device_id_type=MESH)
                low_like.wait_recv()

            @pl.when(jnp.logical_not(low_if))
            def _():
                dst_buf[0] = jnp.zeros(dst_buf.shape[1:], dst_buf.dtype)

            @pl.when(jnp.logical_not(high_if))
            def _():
                dst_buf[1] = jnp.zeros(dst_buf.shape[1:], dst_buf.dtype)

        return finish

    def device_of(index):
        return {"space": lax.div(index, n), "mp": lax.rem(index, n)}

    finish8 = halo(
        send8, halo8, 0,
        place > 0, device_of(jnp.maximum(place - 1, 0)),
        place < last, device_of(jnp.minimum(place + 1, last)),
    )
    zero = normed[0:wide]
    one = normed[wide:]

    def fill8(at, count, even, odd):
        v8[0, at : at + count, :] = shifted(odd, 1, cols).astype(jnp.bfloat16)
        v8[1, at : at + count, :] = even.astype(jnp.bfloat16)
        v8[2, at : at + count, :] = odd.astype(jnp.bfloat16)
        v8[3, at : at + count, :] = shifted(even, -1, cols).astype(jnp.bfloat16)

    fill8(cols, wide, zero, one)

    share_with_core(0)
    for k in peers:
        sends[COARSE, k].wait_recv()
    coarse = cbuf[...].astype(jnp.float32).T
    levels = (
        (1, rows, cols, x16, send16, halo16, w1, coarse[:px], 0),
        (2, r2, c2, x32, send32, halo32, w2, coarse[px:], px),
    )

    def fill(x, at, count, values, width):
        x[0, at : at + count, :] = shifted(values, 1, width).astype(jnp.bfloat16)
        x[1, at : at + count, :] = values.astype(jnp.bfloat16)
        x[2, at : at + count, :] = shifted(values, -1, width).astype(jnp.bfloat16)

    finishes = []
    for level, height, width, x, snd, hal, w, values, at in levels:
        out = lane_norm(values, gain[2 * level : 2 * level + 1, :], shift[2 * level : 2 * level + 1, :])
        fill(x, width, height * width, out, width)
        snd[0] = out[:width].astype(jnp.bfloat16)
        snd[1] = out[height * width - width :].astype(jnp.bfloat16)
        finishes.append(halo(
            snd, hal, level,
            band > 0, {"space": jnp.maximum(band - 1, 0)},
            band < bands - 1, {"space": jnp.minimum(band + 1, bands - 1)},
        ))
    finish8()
    fill8(0, cols, halo8[0, 0:cols].astype(jnp.float32), halo8[0, cols:].astype(jnp.float32))
    fill8(cols + wide, cols, halo8[1, 0:cols].astype(jnp.float32), halo8[1, cols:].astype(jnp.float32))
    locals_[4].wait()
    for k in peers:
        stage_three[0, k].wait_recv()
    part_px = wide // 2
    for part_at in range(2):
        result = jnp.zeros((2 * part_px, neck), jnp.float32)
        for tap in range(9):
            r, q = tap // 3, tap % 3
            at = r * cols + part_at * part_px
            window = v8[q : q + 2, at : at + part_px, :].reshape(2 * part_px, neck)
            result = result + nt(window, w0[tap])
        out = lane_norm(result.astype(jnp.bfloat16), gain[1:2, :], shift[1:2, :])
        for g in range(neck // 128):
            for b in range(2):
                inter[g, pl.ds(2 * part_at * part_px + b, part_px, stride=2), :] = out[
                    b * part_px : (b + 1) * part_px, g * 128 : (g + 1) * 128
                ]
        for g in range(neck // 128):
            osend[part_at, g * 128 : (g + 1) * 128, :] = inter[
                g, part_at * wide : (part_at + 1) * wide, :
            ].T.astype(jnp.bfloat16)
        cells = pl.ds(pl.multiple_of((2 * me + part_at) * wide, wide), wide)
        launch(
            FINAL + part_at,
            lambda k: (
                osend.at[part_at, pl.ds(pl.multiple_of(at_mp(k) * own, own), own)],
                o8.at[:, cells],
            ),
        )
        o8[:, cells] = osend[part_at, mine, :]

    maps = []
    locals_[5].wait()
    locals_[6].wait()
    for (level, height, width, x, snd, hal, w, values, at), done in zip(levels, finishes):
        done()
        fill(x, 0, width, hal[0].astype(jnp.float32), width)
        fill(x, (height + 1) * width, width, hal[1].astype(jnp.float32), width)
        result = jnp.zeros((own, height * width), jnp.float32)
        for tap in range(9):
            r, q = tap // 3, tap % 3
            result = result + nt(
                w[tap], x[q, r * width : (r + height) * width, :]
            )
        result = result.astype(jnp.bfloat16).astype(jnp.float32)
        span = slice(at, at + height * width)
        mbuf[0, 0:1, span] = jnp.sum(result, axis=0, keepdims=True)
        mbuf[0, 1:2, span] = jnp.sum(result * result, axis=0, keepdims=True)
        maps.append(result)
    launch(MOMENT, lambda k: (mbuf.at[0], mbuf.at[k]))

    lane = lax.broadcasted_iota(jnp.int32, (own, neck), 1)
    row = lax.broadcasted_iota(jnp.int32, (own, neck), 0)
    chosen = lane == row + me * own

    def own_column(table, index):
        return jnp.sum(
            jnp.where(chosen, table[index : index + 1, :], 0.0), axis=1, keepdims=True
        )

    for k in peers:
        sends[MOMENT, k].wait_recv()
    moments = mbuf[0]
    for k in peers:
        moments = moments + mbuf[k]
    moments = moments / neck
    for (level, height, width, x, snd, hal, w, values, at), result in zip(levels, maps):
        span = slice(at, at + height * width)
        center = moments[0:1, span]
        spread = moments[1:2, span] - center * center
        scaled = (result - center) * lax.rsqrt(spread + EPSILON)
        final = (
            scaled * own_column(gain, 2 * level + 1) + own_column(shift, 2 * level + 1)
        ).astype(jnp.bfloat16)
        if level == 1:
            o16[...] = final
        else:
            o32[...] = final
            count = o64.shape[0]
            wide2 = c2 // 2
            cell = lax.broadcasted_iota(jnp.int32, (count, px2), 1)
            target = lax.broadcasted_iota(jnp.int32, (count, px2), 0)
            wanted = lax.div(target, wide2) * (2 * c2) + 2 * lax.rem(target, wide2)
            pick = jnp.where(cell == wanted, 1.0, 0.0).astype(jnp.bfloat16)
            o64[...] = nt(pick, final).astype(jnp.bfloat16)

    for copy in (*first.values(), *relay, *stage_one.values(), *stage_two.values(), *stage_three.values()):
        copy.wait_send()
    for kind in range(KINDS):
        for k in peers:
            sends[kind, k].wait_send()
    for k in peers:
        sends[FINAL, k].wait_recv()
        sends[FINAL + 1, k].wait_recv()


def hand_over(*refs):
    count = len(refs) // 2
    for source, target in zip(refs[:count], refs[count:]):
        target[...] = source[...]


def fused(features, deconv_weight, deconv_bias, lateral_eight, lateral_coarse, output_conv,
          norm_gain, norm_shift):
    n = lax.axis_size("mp")
    bands = lax.axis_size("space")
    rows, cols, depth = features.shape
    full = deconv_weight.shape[2]
    hown = deconv_weight.shape[1]
    own = lateral_eight.shape[0]
    neck, half = own * n, hown * n
    layers = lax.axis_size("dp")
    px, px2 = rows * cols, rows * cols // 4
    wide = 2 * (rows // n) * cols
    bf, f32 = jnp.bfloat16, jnp.float32
    vmem = pl.BlockSpec(memory_space=pltpu.VMEM)
    hbm = pl.BlockSpec(memory_space=pl.ANY)
    shapes = [
        ((n, px, depth), bf), ((4 * hown, full), bf), ((2 * own, full), bf),
        ((neck, half), bf), ((9, neck, neck), bf), ((9, own, neck), bf), ((9, own, neck), bf),
        ((px, 4 * hown), f32), ((px // 2, 128), f32), ((n, 2 * wide, hown), bf),
        ((n, 2 * wide, hown), bf), ((neck, px + px2), bf),
        ((4, wide + 2 * cols, neck), bf), ((3, px + 2 * cols, neck), bf),
        ((3, px2 + cols, neck), bf),
        ((2, 2 * cols, neck), bf), ((2, cols, neck), bf), ((2, cols // 2, neck), bf),
        ((2, 2 * cols, neck), bf), ((2, cols, neck), bf), ((2, cols // 2, neck), bf),
        ((n, 8, px + px2), f32), ((neck // 128, 2 * wide, 128), f32), ((2, neck, wide), bf),
    ]
    results = pl.pallas_call(
        functools.partial(pyramid_kernel, n, bands, rows, cols, neck, half),
        out_shape=[
            jax.ShapeDtypeStruct((own, 4 * px), bf), jax.ShapeDtypeStruct((own, px), bf),
            jax.ShapeDtypeStruct((own, px2), bf), jax.ShapeDtypeStruct((px2 // 4, own), bf),
        ],
        in_specs=[hbm, hbm, vmem, hbm, hbm, hbm, vmem, vmem],
        out_specs=[vmem] * 4,
        scratch_shapes=[pltpu.VMEM(s, d) for s, d in shapes] + [
            pltpu.SemaphoreType.DMA((KINDS, n)), pltpu.SemaphoreType.DMA((KINDS, n)),
            pltpu.SemaphoreType.DMA((7,)), pltpu.SemaphoreType.DMA((3, 2)),
            pltpu.SemaphoreType.DMA((3, 2)),
            pltpu.SemaphoreType.DMA((n, 2)), pltpu.SemaphoreType.DMA((n, 2)),
            pltpu.SemaphoreType.DMA((2, layers + 1, n)), pltpu.SemaphoreType.DMA((2, layers + 1, n)),
        ],
        compiler_params=pltpu.CompilerParams(
            collective_id=0, has_side_effects=True, vmem_limit_bytes=56 << 20
        ),
    )(
        features.reshape(px, depth), deconv_weight.reshape(4 * hown, full),
        deconv_bias.reshape(1, hown), lateral_eight, lateral_coarse.reshape(2 * own, full),
        output_conv.transpose(0, 2, 1, 3), norm_gain, norm_shift,
    )
    eight, sixteen, thirty, sixty = pl.pallas_call(
        hand_over,
        out_shape=[jax.ShapeDtypeStruct(r.shape, r.dtype) for r in results],
        in_specs=[vmem] * 4,
        out_specs=[vmem] * 4,
    )(*results)
    return eight, sixteen, thirty, sixty.T


def per_device(features, deconv_weight, *rest):
    n = lax.axis_size("mp")
    rows, cols, depth = features.shape
    aligned = depth % 128 == 0 and deconv_weight.shape[1] % 128 == 0
    bands, layers = lax.axis_size("space"), lax.axis_size("dp")
    own, neck = rest[1].shape[0], rest[3].shape[3]
    aligned = aligned and n == 4 and bands == 2 and own % (16 * layers) == 0 and neck % (128 * bands) == 0
    if aligned and rows % n == 0 and rows % 4 == 0 and cols % 64 == 0:
        return tuple(fused(features, deconv_weight, *rest))
    return channel_pyramid(features, deconv_weight, *rest)


def solution(mesh):
    return jax.shard_map(
        per_device,
        mesh=mesh,
        in_specs=(
            P(("dp", "space"), None, "mp"),
            P(None, "mp", None),
            P("mp"),
            P("mp", None),
            P(None, "mp", None),
            P(None, "mp", None, None),
            P(),
            P(),
        ),
        out_specs=(
            P("mp", ("dp", "space")),
            P("mp", ("dp", "space")),
            P("mp", ("dp", "space")),
            P("mp", ("dp", "space")),
        ),
        check_vma=False,
    )
```
